256 devices in a mesh: dp: 64 (over z, x, core), tensor: 4 (over y).
Axes of the slice: x: 4, y: 4, z: 8, core: 2. Of those that a mesh axis runs over, the one named last changes fastest.
Arguments:
- attn_out: bfloat16 [65536, 8192], P('dp', 'tensor'), may hold values from -8 to 8, as said below
- grad_out: bfloat16 [65536, 2048], P('dp'), may hold values from -0.35327148 to 0.35327148, as said below
- grad_acc: float32 [2048, 8192], P('dp', 'tensor'), may hold values from -1060 to 1060, as said below
- master_weight: float32 [2048, 8192], P('dp', 'tensor'), may hold values from -60 to 60, as said below
- moment_m: float32 [2048, 8192], P('dp', 'tensor'), may hold values from -4 to 4
- moment_v: float32 [2048, 8192], P('dp', 'tensor'), may hold values from 0.001 to 0.01
Outputs:
- moment_new: float32 [2048, 8192], P('dp', 'tensor')
- second_new: float32 [2048, 8192], P('dp', 'tensor')
- scaled_step: float32 [2048, 8192], P('dp', 'tensor')
The draws below stay inside these ranges and needn't reach their ends.
Inputs may be any that keep to these rules, and one draw needn't show every extreme that they name: `attn_out`: finite values. `grad_out`: finite values. `grad_acc`: finite values. `master_weight`: finite values.
All inputs are finite; a program needn't handle non-finite values.
Results may differ from the reference program's by a relative error of at most 0.0003.
Values sent between devices are 32-bit elements; how exact they have to be, the bound alone decides.
No kernel may reach another device: no remote copies, remote signals or barrier semaphores. Data moves between devices by JAX's collectives and lax.ppermute only.
A program may use at most 128 MiB of HBM per device.

```python
import math
import jax
import jax.numpy as jnp
from jax import lax

ROWS_DEV = 8
TOK_DEV = 1024
TOKENS = 65536
IN_FEATURES = 8192
OUT_ROWS = 2048
N_TENSOR = 4


def loguniform_draw(key, count, low, high):
    return jnp.exp(jax.random.uniform(key, (count,), jnp.float32, math.log(low), math.log(high)))


def shared_factors(key):
    subkeys = jax.random.split(jax.random.fold_in(key, 101), 4)
    token_sign = jnp.where(jax.random.bernoulli(subkeys[0], 0.5, (TOKENS,)), 1.0, -1.0).astype(jnp.float32)
    row_dir = jnp.clip(jax.random.normal(subkeys[1], (OUT_ROWS,), jnp.float32), -4.0, 4.0)
    col_dir = jnp.clip(jax.random.normal(subkeys[2], (IN_FEATURES,), jnp.float32), -4.0, 4.0)
    pairing = jax.random.permutation(subkeys[3], TOKENS // TOK_DEV)
    return (token_sign, row_dir, col_dir, pairing)


def draw_attn_out(key, part):
    token_sign, row_dir, col_dir, pairing = shared_factors(key)
    noise_key = jax.random.fold_in(key, 31)
    noise = jnp.clip(jax.random.normal(noise_key, (TOKENS, IN_FEATURES), jnp.float32), -6.0, 6.0)
    strength = 0.5
    return (noise + strength * token_sign[:, None] * col_dir[None, :]).astype(jnp.bfloat16)


def draw_grad_out(key, part):
    token_sign, row_dir, col_dir, pairing = shared_factors(key)
    noise_key = jax.random.fold_in(key, 37)
    sigma = 5.0 / math.sqrt(TOKENS)
    noise = jnp.clip(jax.random.normal(noise_key, (TOKENS, OUT_ROWS), jnp.float32), -6.0, 6.0)
    token_block = jnp.arange(TOKENS) // TOK_DEV
    row_block = jnp.arange(OUT_ROWS) // (ROWS_DEV * N_TENSOR)
    paired = pairing[token_block][:, None] == row_block[None, :]
    factor = jnp.where(paired, 3.0, 1.0).astype(jnp.float32)
    coherent = 28.0 / TOKENS * token_sign[:, None] * row_dir[None, :]
    return (sigma * noise * factor + coherent).astype(jnp.bfloat16)


def draw_grad_acc(key, part):
    subkeys = jax.random.split(jax.random.fold_in(key, 11), 3)
    row_ramp = 3.0 ** (jnp.arange(OUT_ROWS, dtype=jnp.float32) / max(OUT_ROWS - 1, 1))
    base_values = jnp.clip(jax.random.normal(subkeys[0], (OUT_ROWS, IN_FEATURES), jnp.float32), -6.0, 6.0)
    row_factor = loguniform_draw(subkeys[1], OUT_ROWS, 1.0, 4.0)
    column_factor = loguniform_draw(subkeys[2], IN_FEATURES, 1.0, 10.0)
    values = base_values * (row_ramp * row_factor)[:, None] * column_factor[None, :]
    return values.astype(jnp.float32)


def draw_master_weight(key, part):
    subkeys = jax.random.split(jax.random.fold_in(key, 23), 3)
    base_values = jnp.clip(jax.random.normal(subkeys[0], (OUT_ROWS, IN_FEATURES), jnp.float32), -6.0, 6.0)
    row_factor = loguniform_draw(subkeys[1], OUT_ROWS, 1.0, 10.0)
    column_factor = loguniform_draw(subkeys[2], IN_FEATURES, 1.0, 10.0)
    return (0.1 * base_values * row_factor[:, None] * column_factor[None, :]).astype(jnp.float32)


def shard_levels(key, dims, pieces, least, top_value):
    level = 1.0
    for axis_at, parts in pieces:
        draws = jax.random.uniform(jax.random.fold_in(jax.random.fold_in(key, 6), axis_at), (parts,), jnp.float32, least / len(pieces), top_value / len(pieces))
        level = level * jnp.repeat(jnp.exp(draws), dims[axis_at] // parts).reshape((-1,) + (1,) * (len(dims) - 1 - axis_at))
    return level


def gaussian(own_key, shape, deviation, limit, pieces=(), kind=jnp.bfloat16):
    factor_of = shard_levels(own_key, shape, pieces, -0.22, 0.18) if pieces else 1.0
    result = jax.random.normal(own_key, shape, jnp.float32) * deviation * factor_of
    return jnp.minimum(jnp.maximum(result, -limit), limit).astype(kind)


def setup_inputs(seed: int = 0) -> dict:
    splits = jax.random.split(jax.random.key(seed), 7)
    attn_out = draw_attn_out(jax.random.fold_in(splits[6], 71), 0)
    grad_out = draw_grad_out(jax.random.fold_in(splits[6], 71), 0)
    grad_acc = draw_grad_acc(jax.random.fold_in(splits[6], 71), 0)
    master_weight = draw_master_weight(jax.random.fold_in(splits[6], 71), 0)
    moment_m = gaussian(splits[4], (OUT_ROWS, IN_FEATURES), 0.3, 4.0, ((0, 64), (1, 4)), jnp.float32)
    moment_v = jnp.clip(jnp.exp(math.log(0.01) - 2.30258502 * jax.random.uniform(splits[5], (OUT_ROWS, IN_FEATURES), jnp.float32) ** shard_levels(splits[5], (OUT_ROWS, IN_FEATURES), ((0, 64), (1, 4)), -0.2, 0.2)), 0.001, 0.01)
    return dict(attn_out=attn_out, grad_out=grad_out, grad_acc=grad_acc, master_weight=master_weight, moment_m=moment_m, moment_v=moment_v)


beta_first = 0.9
beta_second = 0.999
weight_decay = 0.01
epsilon = 1e-06

def lamb_moments(gradient, divisor, weight, moment, second):
    clipped = gradient / divisor
    moment_new = beta_first * moment + (1.0 - beta_first) * clipped
    second_new = beta_second * second + (1.0 - beta_second) * clipped * clipped
    update = moment_new / (jnp.sqrt(second_new) + epsilon) + weight_decay * weight
    return (moment_new, second_new, update)

def reference(attn_out, grad_out, grad_acc, master_weight, moment_m, moment_v):
    batch_grad = lax.dot_general(grad_out, attn_out, (((0,), (0,)), ((), ())), preferred_element_type=jnp.float32)
    gradient = grad_acc + batch_grad
    grad_rms = jnp.sqrt(jnp.sum(gradient * gradient) / (OUT_ROWS * IN_FEATURES) + epsilon)
    moment_new, second_new, update = lamb_moments(gradient, grad_rms, master_weight, moment_m, moment_v)
    weight_norm = jnp.sqrt(lax.optimization_barrier(jnp.sum(master_weight * master_weight, axis=1, keepdims=True)))
    update_norm = jnp.sqrt(lax.optimization_barrier(jnp.sum(update * update, axis=1, keepdims=True)))
    scaled_step = weight_norm / (update_norm + epsilon) * update
    return (moment_new, second_new, scaled_step)
```

```python
import functools

import jax
import jax.numpy as jnp
from jax import lax
from jax.experimental import pallas as pl
from jax.experimental.pallas import tpu as pltpu
from jax.sharding import Mesh, PartitionSpec as P

beta_first = 0.9
beta_second = 0.999
weight_decay = 0.01
epsilon = 1e-06

DP = ("z", "x", "c")
NZ, NX = 8, 4
COLS_Z = 896


def product_kernel(blocks, pieces, z_major, where_ref, lhs_ref, rhs_ref, *refs):
    outs, acc = refs[:-1], refs[-1]
    step = pl.program_id(0)
    acc[...] = lax.dot_general(
        lhs_ref[...], rhs_ref[...], (((0,), (0,)), ((), ())), preferred_element_type=jnp.float32
    )
    x, c = where_ref[1], where_ref[2]
    for p, offsets in enumerate(pieces):
        keep_ref, send_ref = outs[2 * p], outs[2 * p + 1]
        for i, kx in enumerate(offsets):
            row = lax.rem(x + kx, NX) * 64
            keep = acc[pl.ds(pl.multiple_of(row + c * 32, 32), 32), :]
            send = acc[pl.ds(pl.multiple_of(row + (1 - c) * 32, 32), 32), :]
            if z_major:
                keep_ref[0, i] = keep
                send_ref[0, i] = send
            else:
                keep_ref[i, 0] = keep
                send_ref[i, 0] = send


def product(where, grad_out, attn_part, kz_list, pieces, z_major):
    tokens, cols = attn_part.shape
    steps = len(kz_list)
    out_shape, out_specs = [], []
    for offsets in pieces:
        for _ in range(2):
            if z_major:
                out_shape.append(jax.ShapeDtypeStruct((steps, len(offsets), 32, cols), jnp.float32))
                out_specs.append(pl.BlockSpec((1, len(offsets), 32, cols), lambda k, s: (k, 0, 0, 0)))
            else:
                out_shape.append(jax.ShapeDtypeStruct((len(offsets), steps, 32, cols), jnp.float32))
                out_specs.append(pl.BlockSpec((len(offsets), 1, 32, cols), lambda k, s: (0, k, 0, 0)))
    first = kz_list[0]
    stride = (kz_list[1] - first) if steps > 1 else 0
    assert list(kz_list) == [first + stride * k for k in range(steps)]
    total_rows = 256 * steps
    return pl.pallas_call(
        functools.partial(product_kernel, kz_list, pieces, z_major),
        grid_spec=pltpu.PrefetchScalarGridSpec(
            num_scalar_prefetch=1,
            grid=(steps,),
            in_specs=[
                pl.BlockSpec((tokens, 256), lambda k, s: (0, lax.rem(s[0] + first + stride * k, NZ))),
                pl.BlockSpec((tokens, cols), lambda k, s: (0, 0)),
            ],
            out_specs=out_specs,
            scratch_shapes=[pltpu.VMEM((256, cols), jnp.float32)],
        ),
        out_shape=out_shape,
        compiler_params=pltpu.CompilerParams(vmem_limit_bytes=24 << 20),
        cost_estimate=pl.CostEstimate(
            flops=2 * total_rows * tokens * cols,
            bytes_accessed=2 * tokens * (cols + total_rows) + 4 * total_rows * cols,
            transcendentals=0,
        ),
    )(where, grad_out, attn_part)


def shift(value, axis, by):
    n = {"z": NZ, "x": NX, "c": 2, "y": 4}[axis]
    return lax.ppermute(value, axis, [(i, (i + by) % n) for i in range(n)])


def ring_sum(term, axis, n):
    half = n // 2
    far = term(half)
    cut = far.shape[0] // 2
    up, down = far[:cut], far[cut:]
    rest = [(0, 0, 0)] * (far.ndim - 1)
    zero = jnp.float32(0)
    for k in range(half - 1, -1, -1):
        up, down = shift(up, axis, 1), shift(down, axis, -1)
        if k == half - 1:
            size = far.shape[0]
            up = lax.pad(up, zero, [(0, size - cut, 0)] + rest)
            down = lax.pad(down, zero, [(cut, 0, 0)] + rest)
        if k:
            up, down = term(k) + up, term(n - k) + down
    return term(0) + up + down


def everywhere(tile, axes):
    for axis in axes:
        if axis == "z":
            tile = tile + shift(tile, "z", 2) + shift(tile, "z", 4) + shift(tile, "z", 6)
            tile = tile + shift(tile, "z", 1)
        elif axis == "c":
            tile = tile + shift(tile, "c", 1)
        else:
            tile = tile + shift(tile, axis, 1) + shift(tile, axis, 2) + shift(tile, axis, 3)
    return tile


def shards(attn_out, grad_out, grad_acc, master_weight, moment_m, moment_v):
    entry_count = 2048 * 8192
    where = jnp.stack([lax.axis_index(a) for a in DP]).astype(jnp.int32)
    attn_z, attn_x = attn_out[:, :COLS_Z], attn_out[:, COLS_Z:]

    weight_square = jnp.sum((master_weight * master_weight).reshape(32, 16, 128), axis=1)
    weight_norm = jnp.sqrt(jnp.sum(everywhere(weight_square, ("y",)), axis=1, keepdims=True))

    terms_z, terms_x = {}, {}
    all_x = tuple(range(NX))
    for kz_list in ((4,), (3, 5), (2, 6), (7, 8, 9)):
        keep, send = product(where, grad_out, attn_z, kz_list, (all_x,), True)
        other = shift(send, "c", 1)
        for i, kz in enumerate(kz_list):
            terms_z[kz % NZ] = (keep, other, i)
    pieces = ((2,), (1, 3), (0,))
    outs = product(where, grad_out, attn_x, tuple(range(NZ)), pieces, False)
    for p, offsets in enumerate(pieces):
        keep, other = outs[2 * p], shift(outs[2 * p + 1], "c", 1)
        for i, kx in enumerate(offsets):
            terms_x[kx] = (keep, other, i)

    def term_z(k):
        keep, other, i = terms_z[k]
        return keep[i] + other[i]

    def term_x(k):
        keep, other, i = terms_x[k]
        return keep[i] + other[i]

    sum_z = ring_sum(term_z, "z", NZ)
    sum_x = ring_sum(term_x, "x", NX)
    batch_z = ring_sum(lambda k: sum_z[k], "x", NX)
    batch_x = ring_sum(lambda k: sum_x[k], "z", NZ)
    gradient = grad_acc + jnp.concatenate([batch_z, batch_x], axis=1)

    energy = jnp.sum((gradient * gradient).reshape(4, 8, 16, 128), axis=(0, 2))
    energy = jnp.sum(everywhere(energy, ("c", "y", "x", "z")))
    divisor = jnp.sqrt(energy / entry_count + epsilon)
    clipped = gradient / divisor
    moment_new = beta_first * moment_m + (1.0 - beta_first) * clipped
    second_new = beta_second * moment_v + (1.0 - beta_second) * clipped * clipped
    update = moment_new / (jnp.sqrt(second_new) + epsilon) + weight_decay * master_weight
    update_square = jnp.sum((update * update).reshape(32, 16, 128), axis=1)
    update_norm = jnp.sqrt(jnp.sum(everywhere(update_square, ("y",)), axis=1, keepdims=True))
    return moment_new, second_new, weight_norm / (update_norm + epsilon) * update


def solution(mesh):
    fine = Mesh(mesh.devices.reshape(NZ, NX, 2, 4), DP + ("y",))
    split = P(DP, "y")
    return jax.shard_map(
        shards, mesh=fine, in_specs=(split, P(DP, None)) + (split,) * 4, out_specs=(split,) * 3, check_vma=False
    )
```

```python
import functools

import jax
import jax.numpy as jnp
from jax import lax
from jax.experimental import pallas as pl
from jax.experimental.pallas import tpu as pltpu
from jax.sharding import Mesh, PartitionSpec as P

beta_first = 0.9
beta_second = 0.999
weight_decay = 0.01
epsilon = 1e-06

DP = ("z", "x", "c")
NZ, NX = 8, 4
COLS_Z = 1152


def product_kernel(pieces, z_major, where_ref, lhs_ref, rhs_ref, *refs):
    outs, acc = refs[:-1], refs[-1]
    acc[...] = lax.dot_general(
        lhs_ref[...], rhs_ref[...], (((0,), (0,)), ((), ())), preferred_element_type=jnp.float32
    )
    x, c = where_ref[1], where_ref[2]
    for p, offsets in enumerate(pieces):
        keep_ref, send_ref = outs[2 * p], outs[2 * p + 1]
        for i, kx in enumerate(offsets):
            row = lax.rem(x + kx, NX) * 64
            keep = acc[pl.ds(pl.multiple_of(row + c * 32, 32), 32), :]
            send = acc[pl.ds(pl.multiple_of(row + (1 - c) * 32, 32), 32), :]
            if z_major:
                keep_ref[0, i] = keep
                send_ref[0, i] = send
            else:
                keep_ref[i, 0] = keep
                send_ref[i, 0] = send


def product(where, grad_out, attn_out, start, cols, kz_list, pieces, z_major):
    tokens = attn_out.shape[0]
    steps = len(kz_list)
    out_shape, out_specs = [], []
    for offsets in pieces:
        for _ in range(2):
            if z_major:
                out_shape.append(jax.ShapeDtypeStruct((steps, len(offsets), 32, cols), jnp.float32))
                out_specs.append(pl.BlockSpec((1, len(offsets), 32, cols), lambda k, s: (k, 0, 0, 0)))
            else:
                out_shape.append(jax.ShapeDtypeStruct((len(offsets), steps, 32, cols), jnp.float32))
                out_specs.append(pl.BlockSpec((len(offsets), 1, 32, cols), lambda k, s: (0, k, 0, 0)))
    first = kz_list[0]
    stride = (kz_list[1] - first) if steps > 1 else 0
    assert list(kz_list) == [first + stride * k for k in range(steps)]
    total_rows = 256 * steps
    return pl.pallas_call(
        functools.partial(product_kernel, pieces, z_major),
        grid_spec=pltpu.PrefetchScalarGridSpec(
            num_scalar_prefetch=1,
            grid=(steps,),
            in_specs=[
                pl.BlockSpec((tokens, 256), lambda k, s: (0, lax.rem(s[0] + first + stride * k, NZ))),
                pl.BlockSpec((pl.Element(tokens), pl.Element(cols)), lambda k, s: (0, start)),
            ],
            out_specs=out_specs,
            scratch_shapes=[pltpu.VMEM((256, cols), jnp.float32)],
        ),
        out_shape=out_shape,
        compiler_params=pltpu.CompilerParams(vmem_limit_bytes=24 << 20),
        cost_estimate=pl.CostEstimate(
            flops=2 * total_rows * tokens * cols,
            bytes_accessed=2 * tokens * (cols + total_rows) + 4 * total_rows * cols,
            transcendentals=0,
        ),
    )(where, grad_out, attn_out)


def shift(value, axis, by):
    n = {"z": NZ, "x": NX, "c": 2, "y": 4}[axis]
    return lax.ppermute(value, axis, [(i, (i + by) % n) for i in range(n)])


def after(value, *others):
    return lax.optimization_barrier((value,) + others)[0]


def ring_sum(term, axis, n, early=None):
    half = n // 2
    far = term(half) if early is None else early
    cut = far.shape[0] // 2
    up, down = far[:cut], far[cut:]
    rest = [(0, 0, 0)] * (far.ndim - 1)
    zero = jnp.float32(0)
    for k in range(half - 1, -1, -1):
        up, down = lax.optimization_barrier((up, down))
        up, down = shift(up, axis, 1), shift(down, axis, -1)
        if k == half - 1:
            size = far.shape[0]
            up = lax.pad(up, zero, [(0, size - cut, 0)] + rest)
            down = lax.pad(down, zero, [(cut, 0, 0)] + rest)
        if k:
            up, down = term(k) + up, term(n - k) + down
    return term(0) + up + down


def sum_over(tile, axes, n):
    copies = jnp.broadcast_to(tile[None], (n,) + tile.shape)
    return jnp.sum(lax.all_to_all(copies, axes, 0, 0, tiled=True), axis=0)


def sum_over_tensor(tile):
    return tile + shift(tile, "y", 1) + shift(tile, "y", 2) + shift(tile, "y", 3)


def shards(attn_out, grad_out, grad_acc, master_weight, moment_m, moment_v):
    entry_count = 2048 * 8192
    where = jnp.stack([lax.axis_index(a) for a in DP]).astype(jnp.int32)
    terms_z, terms_x = {}, {}
    all_x = tuple(range(NX))

    def product_z(where, kz_list):
        keep, send = product(where, grad_out, attn_out, 0, COLS_Z, kz_list, (all_x,), True)
        other = shift(send, "c", 1)
        for i, kz in enumerate(kz_list):
            terms_z[kz % NZ] = (keep, other, i)
        return keep

    def term_z(k):
        keep, other, i = terms_z[k]
        return keep[i] + other[i]

    def term_x(k):
        keep, other, i = terms_x[k]
        return keep[i] + other[i]

    done = product_z(where, (4,))
    done = product_z(after(where, done), (3, 5))
    far_z = lax.optimization_barrier(term_z(4))
    pieces = ((2,), (1, 3), (0,))
    outs = product(
        after(where, done, far_z), grad_out, attn_out, COLS_Z, attn_out.shape[1] - COLS_Z, tuple(range(NZ)), pieces, False
    )
    for p, offsets in enumerate(pieces):
        keep, other = outs[2 * p], shift(outs[2 * p + 1], "c", 1)
        for i, kx in enumerate(offsets):
            terms_x[kx] = (keep, other, i)
    far_x = lax.optimization_barrier(term_x(2))
    done = product_z(after(where, outs[0]), (2, 6))
    done = product_z(after(where, done, far_x), (7, 8, 9))

    weight = after(master_weight, done)
    weight_square = jnp.sum((weight * weight).reshape(32, 16, 128), axis=1)
    weight_norm = jnp.sqrt(jnp.sum(sum_over_tensor(weight_square), axis=1, keepdims=True))

    sum_z = ring_sum(term_z, "z", NZ, far_z)
    sum_x = ring_sum(term_x, "x", NX, far_x)
    sum_z, weight_norm = lax.optimization_barrier((sum_z, weight_norm))
    batch_z = ring_sum(lambda k: sum_z[k], "x", NX)
    batch_x = ring_sum(lambda k: sum_x[k], "z", NZ)
    gradient = grad_acc + jnp.concatenate([batch_z, batch_x], axis=1)

    energy = jnp.sum((gradient * gradient).reshape(4, 8, 16, 128), axis=(0, 2))
    energy = sum_over(sum_over(energy, ("z", "x"), NZ * NX), ("c", "y"), 8)
    divisor = jnp.sqrt(jnp.sum(energy) / entry_count + epsilon)
    clipped = gradient / divisor
    moment_new = beta_first * moment_m + (1.0 - beta_first) * clipped
    second_new = beta_second * moment_v + (1.0 - beta_second) * clipped * clipped
    update = moment_new / (jnp.sqrt(second_new) + epsilon) + weight_decay * master_weight
    update_square = jnp.sum((update * update).reshape(32, 16, 128), axis=1)
    update_norm = jnp.sqrt(jnp.sum(sum_over_tensor(update_square), axis=1, keepdims=True))
    return moment_new, second_new, weight_norm / (update_norm + epsilon) * update


def solution(mesh):
    fine = Mesh(mesh.devices.reshape(NZ, NX, 2, 4), DP + ("y",))
    split = P(DP, "y")
    return jax.shard_map(
        shards, mesh=fine, in_specs=(split, P(DP, None)) + (split,) * 4, out_specs=(split,) * 3, check_vma=False
    )
```

```python
import functools

import jax
import jax.numpy as jnp
from jax import lax
from jax.experimental import pallas as pl
from jax.experimental.pallas import tpu as pltpu
from jax.sharding import Mesh, PartitionSpec as P

beta_first = 0.9
beta_second = 0.999
weight_decay = 0.01
epsilon = 1e-06

DP = ("z", "x", "c")
NZ, NX = 8, 4
SIZE = {"z": NZ, "x": NX}
COLS_Z = 1152


def dot(lhs_ref, rhs_ref, z, start, cols):
    lhs = lhs_ref[:, pl.ds(pl.multiple_of(z * 256, 256), 256)]
    rhs = rhs_ref[:, start : start + cols]
    return lax.dot_general(lhs, rhs, (((0,), (0,)), ((), ())), preferred_element_type=jnp.float32)


def near_x(x, c):
    s = 1 - 2 * c
    ahead = lax.rem(x + s + NX, NX)
    return [(ahead, c), (ahead, 1 - c), (lax.rem(x + 2, NX), c), (x, c)]


def product_z_kernel(hops, cols, where_ref, lhs_ref, rhs_ref, keep_ref, send_ref, acc):
    z, x, c = where_ref[0], where_ref[1], where_ref[2]
    s = 1 - 2 * c
    near, far = near_x(x, c), near_x(x, 1 - c)

    def put(ref, at, groups):
        for i, (gx, gc) in enumerate(groups):
            row = pl.multiple_of(gx * 64 + gc * 32, 32)
            ref[at + i] = acc[pl.ds(row, 32), :]

    at = 0
    for hop in hops:
        acc[...] = dot(lhs_ref, rhs_ref, lax.rem(z + s * hop + NZ, NZ), 0, cols)
        if hop in (0, NZ // 2):
            put(keep_ref, at, near)
            put(send_ref, at, far)
            at += 4
        else:
            put(keep_ref, at, near + far)
            acc[...] = dot(lhs_ref, rhs_ref, lax.rem(z - s * hop + NZ, NZ), 0, cols)
            put(send_ref, at, far + near)
            at += 8


def product_x_kernel(start, cols, where_ref, lhs_ref, rhs_ref, keep2_ref, send2_ref, keep_ref, send_ref, acc):
    z, x, c = where_ref[0], where_ref[1], where_ref[2]
    s = 1 - 2 * c
    ahead, behind, across = lax.rem(x + s + NX, NX), lax.rem(x - s + NX, NX), lax.rem(x + 2, NX)

    def rows(gx, gc):
        return acc[pl.ds(pl.multiple_of(gx * 64 + gc * 32, 32), 32), :]

    def put(slot, group, near):
        if near:
            keep_ref[slot] = rows(ahead, group)
            send_ref[8 + slot] = rows(behind, group)
            keep2_ref[slot] = rows(across, group)
            keep_ref[16 + slot] = rows(x, group)
        else:
            keep_ref[8 + slot] = rows(ahead, group)
            send_ref[slot] = rows(behind, group)
            send2_ref[slot] = rows(across, group)
            send_ref[16 + slot] = rows(x, group)

    @pl.loop(0, NZ)
    def _(t):
        acc[...] = dot(lhs_ref, rhs_ref, lax.rem(z + s * t + NZ, NZ), start, cols)

        @pl.when(jnp.logical_and(t > 0, t < 4))
        def _():
            put(2 * t - 2, c, True)
            put(2 * t - 1, 1 - c, True)

        @pl.when(t > 4)
        def _():
            put(14 - 2 * t, 1 - c, False)
            put(15 - 2 * t, c, False)

        @pl.when(jnp.logical_or(t == 0, t == 4))
        def _():
            slot = jnp.where(t == 4, 6, 7)
            put(slot, c, True)
            put(slot, 1 - c, False)


VMEM = pl.BlockSpec(memory_space=pltpu.VMEM)


def product(kernel, groups, cols, rows, where, grad_out, attn_out):
    return pl.pallas_call(
        kernel,
        in_specs=[pl.BlockSpec(memory_space=pltpu.SMEM), VMEM, VMEM],
        out_specs=[VMEM] * len(groups),
        out_shape=[jax.ShapeDtypeStruct((g, 32, cols), jnp.float32) for g in groups],
        scratch_shapes=[pltpu.VMEM((256, cols), jnp.float32)],
        compiler_params=pltpu.CompilerParams(vmem_limit_bytes=VLIM),
        cost_estimate=pl.CostEstimate(flops=COST * rows * cols, bytes_accessed=COST * rows, transcendentals=0),
    )(where, grad_out, attn_out)


VLIM = 24 << 20
COST = 1


def other_core(value):
    return lax.ppermute(value, "c", [(0, 1), (1, 0)])


def onward(value, axis):
    n = SIZE[axis]
    return lax.ppermute(value, (axis, "c"), [(2 * i + c, 2 * ((i + 1 - 2 * c) % n) + c) for i in range(n) for c in range(2)])


def at_front(part, whole):
    return lax.pad(part, jnp.float32(0), [(0, whole - part.shape[0], 0), (0, 0, 0), (0, 0, 0)])


def ring_sum(blocks, own, axis):
    moving = onward(blocks[0](), axis)
    for block in blocks[1:]:
        here = block()
        if moving.shape != here.shape:
            moving = at_front(moving, here.shape[0])
        moving = onward(here + moving, axis)
    half = moving.shape[0] // 2
    return moving[:half] + other_core(moving[half:]) + own()


def sum_over(tile, axes, n):
    copies = jnp.broadcast_to(tile[None], (n,) + tile.shape)
    return jnp.sum(lax.all_to_all(copies, axes, 0, 0, tiled=True), axis=0)


def after(value, *others):
    return lax.optimization_barrier((value,) + others)[0]


def shards(attn_out, grad_out, grad_acc, master_weight, moment_m, moment_v):
    entry_count = 2048 * 8192
    cols_x = attn_out.shape[1] - COLS_Z
    where = jnp.stack([lax.axis_index(a) for a in DP]).astype(jnp.int32)

    def product_z(where, hops):
        groups = sum(4 if hop in (0, NZ // 2) else 8 for hop in hops)
        return product(
            functools.partial(product_z_kernel, hops, COLS_Z), [groups] * 2, COLS_Z, groups * 64, where, grad_out, attn_out
        )

    def both(keep, send):
        got = other_core(send)
        return lambda lo=0, hi=None: keep[lo:hi] + got[lo:hi]

    pair4 = product_z(where, (4,))
    z4 = both(*pair4)
    pair3 = product_z(after(where, pair4[0]), (3,))
    z3 = both(*pair3)
    z4_there = lax.optimization_barrier(z4())
    keep2, send2, keep, send = product(
        functools.partial(product_x_kernel, COLS_Z, cols_x),
        [8, 8, 24, 24], cols_x, 2048, after(where, pair3[0], z4_there), grad_out, attn_out,
    )
    x2, x10 = both(keep2, send2), both(keep, send)
    pair2 = product_z(after(where, keep2), (2,))
    z2 = both(*pair2)
    x2_there = lax.optimization_barrier(x2())
    pair10 = product_z(after(where, pair2[0], x2_there), (1, 0))
    z10 = both(*pair10)

    sum_z = ring_sum([lambda: z4_there, z3, z2, lambda: z10(0, 8)], lambda: z10(8, 12), "z")
    sum_x = ring_sum([lambda: x2_there, lambda: x10(0, 16)], lambda: x10(16, 24), "x")
    batch_z = ring_sum([lambda: sum_z[2:3], lambda: sum_z[0:2]], lambda: sum_z[3:4], "x")
    batch_x = ring_sum(
        [lambda: sum_x[6:7], lambda: sum_x[4:6], lambda: sum_x[2:4], lambda: sum_x[0:2]], lambda: sum_x[7:8], "z"
    )
    gradient = grad_acc + jnp.concatenate([batch_z[0], batch_x[0]], axis=1)

    energy = jnp.sum((gradient * gradient).reshape(4, 8, 16, 128), axis=(0, 2))
    energy = sum_over(sum_over(energy, ("z", "x"), NZ * NX), ("c", "y"), 8)
    divisor = jnp.sqrt(jnp.sum(energy) / entry_count + epsilon)
    clipped = gradient / divisor
    moment_new = beta_first * moment_m + (1.0 - beta_first) * clipped
    second_new = beta_second * moment_v + (1.0 - beta_second) * clipped * clipped
    update = moment_new / (jnp.sqrt(second_new) + epsilon) + weight_decay * master_weight
    squares = jnp.stack([jnp.sum(master_weight * master_weight, axis=1), jnp.sum(update * update, axis=1)])
    norms = jnp.sqrt(lax.psum(squares, "y"))
    trust = norms[0] / (norms[1] + epsilon)
    return moment_new, second_new, trust[:, None] * update


def solution(mesh):
    fine = Mesh(mesh.devices.reshape(NZ, NX, 2, 4), DP + ("y",))
    split = P(DP, "y")
    return jax.shard_map(
        shards, mesh=fine, in_specs=(split, P(DP, None)) + (split,) * 4, out_specs=(split,) * 3, check_vma=False
    )
```

```python
import functools

import jax
import jax.numpy as jnp
from jax import lax
from jax.experimental import pallas as pl
from jax.experimental.pallas import tpu as pltpu
from jax.sharding import Mesh, PartitionSpec as P

beta_first = 0.9
beta_second = 0.999
weight_decay = 0.01
epsilon = 1e-06

DP = ("z", "x", "c")
NZ, NX = 8, 4
SIZE = {"z": NZ, "x": NX}
COLS_Z = 1280
COLS_X = (512, 256)


def dot(lhs_ref, rhs_ref, z, start, cols):
    lhs = lhs_ref[:, pl.ds(pl.multiple_of(z * 256, 256), 256)]
    rhs = rhs_ref[:, start : start + cols]
    return lax.dot_general(lhs, rhs, (((0,), (0,)), ((), ())), preferred_element_type=jnp.float32)


def near_x(x, c):
    return [(lax.rem(x + k, NX), c) for k in range(NX)]


def product_z_kernel(hops, cols, where_ref, lhs_ref, rhs_ref, keep_ref, send_ref, acc):
    z, x, c = where_ref[0], where_ref[1], where_ref[2]
    s = 1 - 2 * c
    near, far = near_x(x, c), near_x(x, 1 - c)

    def put(ref, at, groups):
        for i, (gx, gc) in enumerate(groups):
            row = pl.multiple_of(gx * 64 + gc * 32, 32)
            ref[at + i] = acc[pl.ds(row, 32), :]

    at = 0
    for hop in hops:
        acc[...] = dot(lhs_ref, rhs_ref, lax.rem(z + s * hop + NZ, NZ), 0, cols)
        if hop in (0, NZ // 2):
            put(keep_ref, at, near)
            put(send_ref, at, far)
            at += 4
        else:
            put(keep_ref, at, near + far)
            acc[...] = dot(lhs_ref, rhs_ref, lax.rem(z - s * hop + NZ, NZ), 0, cols)
            put(send_ref, at, far + near)
            at += 8


def product_far_kernel(cols, where_ref, lhs_hbm, rhs_hbm, keep_ref, send_ref, acc, lhs, rhs, sems):
    z, x, c = where_ref[0], where_ref[1], where_ref[2]
    block = pl.multiple_of(lax.rem(z + NZ // 2, NZ) * 256, 256)
    copies = [
        pltpu.make_async_copy(lhs_hbm.at[:, pl.ds(block, 256)], lhs, sems.at[0]),
        pltpu.make_async_copy(rhs_hbm.at[:, pl.ds(0, cols)], rhs, sems.at[1]),
    ]
    for copy in copies:
        copy.start()
    for copy in copies:
        copy.wait()
    acc[...] = lax.dot_general(lhs[...], rhs[...], (((0,), (0,)), ((), ())), preferred_element_type=jnp.float32)
    for ref, core in ((keep_ref, c), (send_ref, 1 - c)):
        for i, (gx, gc) in enumerate(near_x(x, core)):
            ref[i] = acc[pl.ds(pl.multiple_of(gx * 64 + gc * 32, 32), 32), :]


def product_x_kernel(start, cols, where_ref, lhs_ref, rhs_ref, keep2_ref, send2_ref, keep_ref, send_ref, acc):
    z, x, c = where_ref[0], where_ref[1], where_ref[2]
    s = 1 - 2 * c
    ahead, behind, across = lax.rem(x + s + NX, NX), lax.rem(x - s + NX, NX), lax.rem(x + 2, NX)

    def rows(gx, gc):
        return acc[pl.ds(pl.multiple_of(gx * 64 + gc * 32, 32), 32), :]

    def put(slot, group, near):
        if near:
            keep_ref[slot] = rows(ahead, group)
            send_ref[8 + slot] = rows(behind, group)
            keep2_ref[slot] = rows(across, group)
            keep_ref[16 + slot] = rows(x, group)
        else:
            keep_ref[8 + slot] = rows(ahead, group)
            send_ref[slot] = rows(behind, group)
            send2_ref[slot] = rows(across, group)
            send_ref[16 + slot] = rows(x, group)

    @pl.loop(0, NZ)
    def _(t):
        acc[...] = dot(lhs_ref, rhs_ref, lax.rem(z + s * t + NZ, NZ), start, cols)

        @pl.when(jnp.logical_and(t > 0, t < 4))
        def _():
            put(2 * t - 2, c, True)
            put(2 * t - 1, 1 - c, True)

        @pl.when(t > 4)
        def _():
            put(14 - 2 * t, 1 - c, False)
            put(15 - 2 * t, c, False)

        @pl.when(jnp.logical_or(t == 0, t == 4))
        def _():
            slot = jnp.where(t == 4, 6, 7)
            put(slot, c, True)
            put(slot, 1 - c, False)


VMEM = pl.BlockSpec(memory_space=pltpu.VMEM)


def product(kernel, groups, cols, rows, where, grad_out, attn_out):
    return pl.pallas_call(
        kernel,
        in_specs=[pl.BlockSpec(memory_space=pltpu.SMEM), VMEM, VMEM],
        out_specs=[VMEM] * len(groups),
        out_shape=[jax.ShapeDtypeStruct((g, 32, cols), jnp.float32) for g in groups],
        scratch_shapes=[pltpu.VMEM((256, cols), jnp.float32)],
        compiler_params=pltpu.CompilerParams(vmem_limit_bytes=VLIM),
        cost_estimate=pl.CostEstimate(flops=COST * rows * cols, bytes_accessed=COST * rows, transcendentals=0),
    )(where, grad_out, attn_out)


def product_far(where, grad_out, attn_out):
    tokens, hbm = attn_out.shape[0], pl.BlockSpec(memory_space=pltpu.HBM)
    return pl.pallas_call(
        functools.partial(product_far_kernel, COLS_Z),
        in_specs=[pl.BlockSpec(memory_space=pltpu.SMEM), hbm, hbm],
        out_specs=[VMEM] * 2,
        out_shape=[jax.ShapeDtypeStruct((4, 32, COLS_Z), jnp.float32)] * 2,
        scratch_shapes=[
            pltpu.VMEM((256, COLS_Z), jnp.float32),
            pltpu.VMEM((tokens, 256), jnp.bfloat16),
            pltpu.VMEM((tokens, COLS_Z), jnp.bfloat16),
            pltpu.SemaphoreType.DMA((2,)),
        ],
        compiler_params=pltpu.CompilerParams(vmem_limit_bytes=VLIM),
        cost_estimate=pl.CostEstimate(flops=COST * 256 * COLS_Z, bytes_accessed=COST * 256, transcendentals=0),
    )(where, grad_out, attn_out)


VLIM = 24 << 20
COST = 1


def other_core(value):
    return lax.ppermute(value, "c", [(0, 1), (1, 0)])


def onward(value, axis):
    n = SIZE[axis]
    return lax.ppermute(value, (axis, "c"), [(2 * i + c, 2 * ((i + 1 - 2 * c) % n) + c) for i in range(n) for c in range(2)])


def shift(value, axis, by):
    n = SIZE[axis]
    return lax.ppermute(value, axis, [(i, (i + by) % n) for i in range(n)])


def at_front(part, whole):
    return lax.pad(part, jnp.float32(0), [(0, whole - part.shape[0], 0), (0, 0, 0), (0, 0, 0)])


def sum_over(tile, axes, n):
    copies = jnp.broadcast_to(tile[None], (n,) + tile.shape)
    return jnp.sum(lax.all_to_all(copies, axes, 0, 0, tiled=True), axis=0)


def after(value, *others):
    return lax.optimization_barrier((value, others))[0]


def halves(cols):
    middle = cols // 256 * 128
    return slice(0, middle), slice(middle, cols)


def shards(attn_out, grad_out, grad_acc, master_weight, moment_m, moment_v):
    entry_count = 2048 * 8192
    where = jnp.stack([lax.axis_index(a) for a in DP]).astype(jnp.int32)

    def product_z(where, hops):
        groups = sum(4 if hop in (0, NZ // 2) else 8 for hop in hops)
        return product(
            functools.partial(product_z_kernel, hops, COLS_Z), [groups] * 2, COLS_Z, groups * 64, where, grad_out, attn_out
        )

    def both(pair):
        return pair[0] + pair[1]

    cuts_z = halves(COLS_Z)
    starts_x = (COLS_Z, COLS_Z + COLS_X[0])

    def product_x(where, i):
        return product(
            functools.partial(product_x_kernel, starts_x[i], COLS_X[i]),
            [8, 8, 24, 24], COLS_X[i], 2048, where, grad_out, attn_out,
        )

    def add(here, moving):
        return here + (moving if moving.shape == here.shape else at_front(moving, here.shape[0]))

    far_z = product_far(where, grad_out, attn_out)
    far_z = (far_z[0], other_core(far_z[1]))
    pair3 = product_z(after(where, far_z[0]), (3,))
    pair3 = (pair3[0], other_core(pair3[1]))
    first_z = lax.optimization_barrier(both(far_z))
    z = onward(first_z, "z")
    keep_far, send_far, keep_xa, send_xa = product_x(after(where, pair3[0], first_z), 0)
    far_xa = (keep_far, other_core(send_far))
    z = [z[..., cut] for cut in cuts_z]
    keep_far, send_far, keep_xb, send_xb = product_x(after(where, z, far_xa[1]), 1)
    far_xb = (keep_far, other_core(send_far))

    def hop_z(z, pair, rows):
        a = add(both(pair)[:rows, :, cuts_z[0]], z[0])
        b = add(both(pair)[:rows, :, cuts_z[1]], after(z[1], a))
        return (a, b), [onward(a, "z"), onward(b, "z")]

    step, z = hop_z(z, pair3, 8)
    pair2 = product_z(after(where, step, keep_xb), (2,))
    pair2 = (pair2[0], other_core(pair2[1]))
    first_xa = lax.optimization_barrier(both(far_xa))
    first_xb = after(both(far_xb), first_xa)
    x = [onward(first_xa, "x"), onward(first_xb, "x")]
    pair_xa = (keep_xa, other_core(after(send_xa, first_xa)))
    pair_xb = (keep_xb, other_core(after(send_xb, first_xb, pair_xa[1])))
    pair1 = product_z(after(where, z, first_xb), (1, 0))
    pair1 = (pair1[0], other_core(pair1[1]))
    step, z = hop_z(z, pair2, 8)
    a = add(both(pair_xa)[:16], x[0])
    b = add(both(pair_xb)[:16], after(x[1], a))
    x = [onward(a, "x"), onward(b, "x")]
    step, z = hop_z(z, pair1, 8)

    def swapped(parts, rows):
        return [part[:rows] + other_core(part[rows:]) for part in parts]

    sum_z = jnp.concatenate(swapped(z, 4), axis=2) + both(pair1)[8:12]
    sum_x = jnp.concatenate(
        [part + both(pair)[16:24] for part, pair in zip(swapped(x, 8), (pair_xa, pair_xb))], axis=2
    )

    batch_z = sum_z[0] + sum(shift(sum_z[k], "x", k) for k in (1, 2, 3))
    moving = onward(sum_x[6:7], "z")
    moving = onward(sum_x[4:6] + at_front(moving, 2), "z")
    moving = onward(sum_x[2:4] + moving, "z")
    moving = onward(sum_x[0:2] + moving, "z")
    batch_x = moving[0] + other_core(moving[1]) + sum_x[7]
    gradient = grad_acc + jnp.concatenate([batch_z, batch_x], axis=1)

    energy = jnp.sum((gradient * gradient).reshape(4, 8, 16, 128), axis=(0, 2))
    energy = sum_over(sum_over(energy, ("z", "x"), NZ * NX), ("c", "y"), 8)
    divisor = jnp.sqrt(jnp.sum(energy) / entry_count + epsilon)
    clipped = gradient / divisor
    moment_new = beta_first * moment_m + (1.0 - beta_first) * clipped
    second_new = beta_second * moment_v + (1.0 - beta_second) * clipped * clipped
    update = moment_new / (jnp.sqrt(second_new) + epsilon) + weight_decay * master_weight
    squares = jnp.stack([jnp.sum(master_weight * master_weight, axis=1), jnp.sum(update * update, axis=1)])
    norms = jnp.sqrt(lax.psum(squares, "y"))
    trust = norms[0] / (norms[1] + epsilon)
    return moment_new, second_new, trust[:, None] * update


def solution(mesh):
    fine = Mesh(mesh.devices.reshape(NZ, NX, 2, 4), DP + ("y",))
    split = P(DP, "y")
    return jax.shard_map(
        shards, mesh=fine, in_specs=(split, P(DP, None)) + (split,) * 4, out_specs=(split,) * 3, check_vma=False
    )
```

```python
import functools

import jax
import jax.numpy as jnp
from jax import lax
from jax.experimental import pallas as pl
from jax.experimental.pallas import tpu as pltpu
from jax.sharding import Mesh, PartitionSpec as P

beta_first = 0.9
beta_second = 0.999
weight_decay = 0.01
epsilon = 1e-06

DP = ("z", "x", "c")
NZ, NX = 8, 4
SIZE = {"z": NZ, "x": NX}
COLS_Z = 1280


def dot(lhs_ref, rhs_ref, z, start, cols):
    lhs = lhs_ref[:, pl.ds(pl.multiple_of(z * 256, 256), 256)]
    rhs = rhs_ref[:, start : start + cols]
    return lax.dot_general(lhs, rhs, (((0,), (0,)), ((), ())), preferred_element_type=jnp.float32)


def near_x(x, c):
    return [(lax.rem(x + k, NX), c) for k in range(NX)]


def product_z_kernel(hops, cols, where_ref, lhs_ref, rhs_ref, keep_ref, send_ref, acc):
    z, x, c = where_ref[0], where_ref[1], where_ref[2]
    s = 1 - 2 * c
    near, far = near_x(x, c), near_x(x, 1 - c)

    def put(ref, at, groups):
        for i, (gx, gc) in enumerate(groups):
            row = pl.multiple_of(gx * 64 + gc * 32, 32)
            ref[at + i] = acc[pl.ds(row, 32), :]

    at = 0
    for hop in hops:
        acc[...] = dot(lhs_ref, rhs_ref, lax.rem(z + s * hop + NZ, NZ), 0, cols)
        if hop in (0, NZ // 2):
            put(keep_ref, at, near)
            put(send_ref, at, far)
            at += 4
        else:
            put(keep_ref, at, near + far)
            acc[...] = dot(lhs_ref, rhs_ref, lax.rem(z - s * hop + NZ, NZ), 0, cols)
            put(send_ref, at, far + near)
            at += 8


def product_x_kernel(start, cols, where_ref, lhs_ref, rhs_ref, keep2_ref, send2_ref, keep_ref, send_ref, acc):
    z, x, c = where_ref[0], where_ref[1], where_ref[2]
    s = 1 - 2 * c
    ahead, behind, across = lax.rem(x + s + NX, NX), lax.rem(x - s + NX, NX), lax.rem(x + 2, NX)

    def rows(gx, gc):
        return acc[pl.ds(pl.multiple_of(gx * 64 + gc * 32, 32), 32), :]

    def put(slot, group, near):
        if near:
            keep_ref[slot] = rows(ahead, group)
            send_ref[8 + slot] = rows(behind, group)
            keep2_ref[slot] = rows(across, group)
            keep_ref[16 + slot] = rows(x, group)
        else:
            keep_ref[8 + slot] = rows(ahead, group)
            send_ref[slot] = rows(behind, group)
            send2_ref[slot] = rows(across, group)
            send_ref[16 + slot] = rows(x, group)

    @pl.loop(0, NZ)
    def _(t):
        acc[...] = dot(lhs_ref, rhs_ref, lax.rem(z + s * t + NZ, NZ), start, cols)

        @pl.when(jnp.logical_and(t > 0, t < 4))
        def _():
            put(2 * t - 2, c, True)
            put(2 * t - 1, 1 - c, True)

        @pl.when(t > 4)
        def _():
            put(14 - 2 * t, 1 - c, False)
            put(15 - 2 * t, c, False)

        @pl.when(jnp.logical_or(t == 0, t == 4))
        def _():
            slot = jnp.where(t == 4, 6, 7)
            put(slot, c, True)
            put(slot, 1 - c, False)


VMEM = pl.BlockSpec(memory_space=pltpu.VMEM)


def product(kernel, groups, cols, rows, where, grad_out, attn_out):
    return pl.pallas_call(
        kernel,
        in_specs=[pl.BlockSpec(memory_space=pltpu.SMEM), VMEM, VMEM],
        out_specs=[VMEM] * len(groups),
        out_shape=[jax.ShapeDtypeStruct((g, 32, cols), jnp.float32) for g in groups],
        scratch_shapes=[pltpu.VMEM((256, cols), jnp.float32)],
        compiler_params=pltpu.CompilerParams(vmem_limit_bytes=VLIM),
        cost_estimate=pl.CostEstimate(flops=COST * rows * cols, bytes_accessed=COST * rows, transcendentals=0),
    )(where, grad_out, attn_out)


VLIM = 24 << 20
COST = 1


def other_core(value):
    return lax.ppermute(value, "c", [(0, 1), (1, 0)])


def onward(value, axis):
    n = SIZE[axis]
    return lax.ppermute(value, (axis, "c"), [(2 * i + c, 2 * ((i + 1 - 2 * c) % n) + c) for i in range(n) for c in range(2)])


def shift(value, axis, by):
    n = SIZE[axis]
    return lax.ppermute(value, axis, [(i, (i + by) % n) for i in range(n)])


def at_front(part, whole):
    return lax.pad(part, jnp.float32(0), [(0, whole - part.shape[0], 0), (0, 0, 0), (0, 0, 0)])


def sum_over(tile, axes, n):
    copies = jnp.broadcast_to(tile[None], (n,) + tile.shape)
    return jnp.sum(lax.all_to_all(copies, axes, 0, 0, tiled=True), axis=0)


def after(value, *others):
    return lax.optimization_barrier((value, others))[0]


def shards(attn_out, grad_out, grad_acc, master_weight, moment_m, moment_v):
    entry_count = 2048 * 8192
    where = jnp.stack([lax.axis_index(a) for a in DP]).astype(jnp.int32)

    def product_z(where, hops):
        groups = sum(4 if hop in (0, NZ // 2) else 8 for hop in hops)
        return product(
            functools.partial(product_z_kernel, hops, COLS_Z), [groups] * 2, COLS_Z, groups * 64, where, grad_out, attn_out
        )

    def both(pair):
        return pair[0] + pair[1]

    cols_x = attn_out.shape[1] - COLS_Z

    def add(here, moving):
        return here + (moving if moving.shape == here.shape else at_front(moving, here.shape[0]))

    pair4 = product_z(where, (4,))
    pair4 = (pair4[0], other_core(pair4[1]))
    pair3 = product_z(after(where, pair4[0]), (3,))
    pair3 = (pair3[0], other_core(pair3[1]))
    first_z = lax.optimization_barrier(both(pair4))
    keep_far, send_far, keep_x, send_x = product(
        functools.partial(product_x_kernel, COLS_Z, cols_x),
        [8, 8, 24, 24], cols_x, 2048, after(where, pair3[0], first_z), grad_out, attn_out,
    )
    next_z = add(both(pair3)[:8], onward(first_z, "z"))
    far_x = (keep_far, after(other_core(send_far), next_z))
    pair2 = product_z(after(where, keep_far, next_z), (2,))
    pair2 = (pair2[0], other_core(pair2[1]))
    first_x = lax.optimization_barrier(both(far_x))
    pair_x = (keep_x, other_core(after(send_x, first_x)))
    pair1 = product_z(after(where, pair2[0], first_x), (1, 0))
    pair1 = (pair1[0], other_core(pair1[1]))

    z = onward(next_z, "z")
    for pair in (pair2, pair1):
        z = onward(add(both(pair)[:8], z), "z")
    sum_z = z[:4] + other_core(z[4:]) + both(pair1)[8:12]
    x = onward(first_x, "x")
    x = onward(add(both(pair_x)[:16], x), "x")
    sum_x = x[:8] + other_core(x[8:]) + both(pair_x)[16:24]

    batch_z = sum_z[0] + sum(shift(sum_z[k], "x", k) for k in (1, 2, 3))
    moving = onward(sum_x[6:7], "z")
    moving = onward(add(sum_x[4:6], moving), "z")
    moving = onward(sum_x[2:4] + moving, "z")
    moving = onward(sum_x[0:2] + moving, "z")
    batch_x = moving[0] + other_core(moving[1]) + sum_x[7]
    gradient = grad_acc + jnp.concatenate([batch_z, batch_x], axis=1)

    energy = jnp.sum((gradient * gradient).reshape(4, 8, 16, 128), axis=(0, 2))
    energy = sum_over(sum_over(energy, ("z", "x"), NZ * NX), ("c", "y"), 8)
    divisor = jnp.sqrt(jnp.sum(energy) / entry_count + epsilon)
    clipped = gradient / divisor
    moment_new = beta_first * moment_m + (1.0 - beta_first) * clipped
    second_new = beta_second * moment_v + (1.0 - beta_second) * clipped * clipped
    update = moment_new / (jnp.sqrt(second_new) + epsilon) + weight_decay * master_weight
    squares = jnp.stack([jnp.sum(master_weight * master_weight, axis=1), jnp.sum(update * update, axis=1)])
    norms = jnp.sqrt(lax.psum(squares, "y"))
    trust = norms[0] / (norms[1] + epsilon)
    return moment_new, second_new, trust[:, None] * update


def solution(mesh):
    fine = Mesh(mesh.devices.reshape(NZ, NX, 2, 4), DP + ("y",))
    split = P(DP, "y")
    return jax.shard_map(
        shards, mesh=fine, in_specs=(split, P(DP, None)) + (split,) * 4, out_specs=(split,) * 3, check_vma=False
    )
```

```python
import functools

import jax
import jax.numpy as jnp
from jax import lax
from jax.experimental import pallas as pl
from jax.experimental.pallas import tpu as pltpu
from jax.sharding import Mesh, PartitionSpec as P

beta_first = 0.9
beta_second = 0.999
weight_decay = 0.01
epsilon = 1e-06

DP = ("z", "x", "c")
NZ, NX = 8, 4
SIZE = {"z": NZ, "x": NX}
COLS_Z = 1152


def dot(lhs_ref, rhs_ref, z, start, cols):
    lhs = lhs_ref[:, pl.ds(pl.multiple_of(z * 256, 256), 256)]
    rhs = rhs_ref[:, start : start + cols]
    return lax.dot_general(lhs, rhs, (((0,), (0,)), ((), ())), preferred_element_type=jnp.float32)


def near_x(x, c):
    return [(lax.rem(x + k, NX), c) for k in range(NX)]


def product_z_kernel(hops, cols, where_ref, lhs_ref, rhs_ref, keep_ref, send_ref, acc):
    z, x, c = where_ref[0], where_ref[1], where_ref[2]
    s = 1 - 2 * c
    near, far = near_x(x, c), near_x(x, 1 - c)

    def put(ref, at, groups):
        for i, (gx, gc) in enumerate(groups):
            row = pl.multiple_of(gx * 64 + gc * 32, 32)
            ref[at + i] = acc[pl.ds(row, 32), :]

    at = 0
    for hop in hops:
        acc[...] = dot(lhs_ref, rhs_ref, lax.rem(z + s * hop + NZ, NZ), 0, cols)
        if hop in (0, NZ // 2):
            put(keep_ref, at, near)
            put(send_ref, at, far)
            at += 4
        else:
            put(keep_ref, at, near + far)
            acc[...] = dot(lhs_ref, rhs_ref, lax.rem(z - s * hop + NZ, NZ), 0, cols)
            put(send_ref, at, far + near)
            at += 8


def product_x_kernel(start, cols, where_ref, lhs_ref, rhs_ref, keep2_ref, send2_ref, keep_ref, send_ref, acc):
    z, x, c = where_ref[0], where_ref[1], where_ref[2]
    s = 1 - 2 * c
    ahead, behind, across = lax.rem(x + s + NX, NX), lax.rem(x - s + NX, NX), lax.rem(x + 2, NX)

    def rows(gx, gc):
        return acc[pl.ds(pl.multiple_of(gx * 64 + gc * 32, 32), 32), :]

    def put(slot, group, near):
        if near:
            keep_ref[slot] = rows(ahead, group)
            send_ref[8 + slot] = rows(behind, group)
            keep2_ref[slot] = rows(across, group)
            keep_ref[16 + slot] = rows(x, group)
        else:
            keep_ref[8 + slot] = rows(ahead, group)
            send_ref[slot] = rows(behind, group)
            send2_ref[slot] = rows(across, group)
            send_ref[16 + slot] = rows(x, group)

    @pl.loop(0, NZ)
    def _(t):
        acc[...] = dot(lhs_ref, rhs_ref, lax.rem(z + s * t + NZ, NZ), start, cols)

        @pl.when(jnp.logical_and(t > 0, t < 4))
        def _():
            put(2 * t - 2, c, True)
            put(2 * t - 1, 1 - c, True)

        @pl.when(t > 4)
        def _():
            put(14 - 2 * t, 1 - c, False)
            put(15 - 2 * t, c, False)

        @pl.when(jnp.logical_or(t == 0, t == 4))
        def _():
            slot = jnp.where(t == 4, 6, 7)
            put(slot, c, True)
            put(slot, 1 - c, False)


VMEM = pl.BlockSpec(memory_space=pltpu.VMEM)


def product(kernel, groups, cols, rows, where, grad_out, attn_out):
    return pl.pallas_call(
        kernel,
        in_specs=[pl.BlockSpec(memory_space=pltpu.SMEM), VMEM, VMEM],
        out_specs=[VMEM] * len(groups),
        out_shape=[jax.ShapeDtypeStruct((g, 32, cols), jnp.float32) for g in groups],
        scratch_shapes=[pltpu.VMEM((256, cols), jnp.float32)],
        compiler_params=pltpu.CompilerParams(vmem_limit_bytes=VLIM),
        cost_estimate=pl.CostEstimate(flops=COST * rows * cols, bytes_accessed=COST * rows, transcendentals=0),
    )(where, grad_out, attn_out)


VLIM = 24 << 20
COST = 1


def other_core(value):
    return lax.ppermute(value, "c", [(0, 1), (1, 0)])


def onward(value, axis):
    n = SIZE[axis]
    return lax.ppermute(value, (axis, "c"), [(2 * i + c, 2 * ((i + 1 - 2 * c) % n) + c) for i in range(n) for c in range(2)])


def shift(value, axis, by):
    n = SIZE[axis]
    return lax.ppermute(value, axis, [(i, (i + by) % n) for i in range(n)])


def at_front(part, whole):
    return lax.pad(part, jnp.float32(0), [(0, whole - part.shape[0], 0), (0, 0, 0), (0, 0, 0)])


def sum_over(tile, axes, n):
    copies = jnp.broadcast_to(tile[None], (n,) + tile.shape)
    return jnp.sum(lax.all_to_all(copies, axes, 0, 0, tiled=True), axis=0)


def after(value, *others):
    return lax.optimization_barrier((value, others))[0]


def shards(attn_out, grad_out, grad_acc, master_weight, moment_m, moment_v):
    entry_count = 2048 * 8192
    where = jnp.stack([lax.axis_index(a) for a in DP]).astype(jnp.int32)

    def product_z(where, hops):
        groups = sum(4 if hop in (0, NZ // 2) else 8 for hop in hops)
        return product(
            functools.partial(product_z_kernel, hops, COLS_Z), [groups] * 2, COLS_Z, groups * 64, where, grad_out, attn_out
        )

    def both(pair):
        return pair[0] + pair[1]

    cols_x = attn_out.shape[1] - COLS_Z

    def add(here, moving):
        return here + (moving if moving.shape == here.shape else at_front(moving, here.shape[0]))

    pair4 = product_z(where, (4,))
    pair4 = (pair4[0], other_core(pair4[1]))
    pair3 = product_z(after(where, pair4[0]), (3,))
    pair3 = (pair3[0], other_core(pair3[1]))
    first_z = lax.optimization_barrier(both(pair4))
    keep_far, send_far, keep_x, send_x = product(
        functools.partial(product_x_kernel, COLS_Z, cols_x),
        [8, 8, 24, 24], cols_x, 2048, after(where, pair3[0], first_z), grad_out, attn_out,
    )
    next_z = add(both(pair3)[:8], onward(first_z, "z"))
    far_x = (keep_far, after(other_core(send_far), next_z))
    pair2 = product_z(after(where, keep_far, next_z), (2,))
    pair2 = (pair2[0], other_core(pair2[1]))
    first_x = lax.optimization_barrier(both(far_x))
    pair_x = (keep_x, other_core(after(send_x, first_x)))
    pair1 = product_z(after(where, pair2[0], first_x), (1, 0))
    pair1 = (pair1[0], other_core(pair1[1]))

    z = onward(next_z, "z")
    for pair in (pair2, pair1):
        z = onward(add(both(pair)[:8], z), "z")
    sum_z = z[:4] + other_core(z[4:]) + both(pair1)[8:12]
    x = onward(first_x, "x")
    x = onward(add(both(pair_x)[:16], x), "x")
    sum_x = x[:8] + other_core(x[8:]) + both(pair_x)[16:24]

    batch_z = sum_z[0] + sum(shift(sum_z[k], "x", k) for k in (1, 2, 3))
    moving = onward(sum_x[6:7], "z")
    moving = onward(add(sum_x[4:6], moving), "z")
    moving = onward(sum_x[2:4] + moving, "z")
    moving = onward(sum_x[0:2] + after(moving, batch_z), "z")
    batch_x = moving[0] + other_core(moving[1]) + sum_x[7]
    gradient = grad_acc + jnp.concatenate([batch_z, batch_x], axis=1)

    energy = jnp.sum((gradient * gradient).reshape(4, 8, 16, 128), axis=(0, 2))
    energy = sum_over(sum_over(energy, ("z", "c"), 16), ("x", "y"), 16)
    divisor = jnp.sqrt(jnp.sum(energy) / entry_count + epsilon)
    clipped = gradient / divisor
    moment_new = beta_first * moment_m + (1.0 - beta_first) * clipped
    second_new = beta_second * moment_v + (1.0 - beta_second) * clipped * clipped
    update = moment_new / (jnp.sqrt(second_new) + epsilon) + weight_decay * master_weight
    squares = jnp.stack([jnp.sum(master_weight * master_weight, axis=1), jnp.sum(update * update, axis=1)])
    norms = jnp.sqrt(lax.psum(squares, "y"))
    trust = norms[0] / (norms[1] + epsilon)
    return moment_new, second_new, trust[:, None] * update


def solution(mesh):
    fine = Mesh(mesh.devices.reshape(NZ, NX, 2, 4), DP + ("y",))
    split = P(DP, "y")
    return jax.shard_map(
        shards, mesh=fine, in_specs=(split, P(DP, None)) + (split,) * 4, out_specs=(split,) * 3, check_vma=False
    )
```

```python
import functools

import jax
import jax.numpy as jnp
from jax import lax
from jax.experimental import pallas as pl
from jax.experimental.pallas import tpu as pltpu
from jax.sharding import Mesh, PartitionSpec as P

beta_first = 0.9
beta_second = 0.999
weight_decay = 0.01
epsilon = 1e-06

DP = ("z", "x", "c")
NZ, NX = 8, 4
SIZE = {"z": NZ, "x": NX}
COLS_Z = 1152


def dot(lhs_ref, rhs_ref, z, start, cols):
    lhs = lhs_ref[:, pl.ds(pl.multiple_of(z * 256, 256), 256)]
    rhs = rhs_ref[:, start : start + cols]
    return lax.dot_general(lhs, rhs, (((0,), (0,)), ((), ())), preferred_element_type=jnp.float32)


def near_x(x, c):
    return [(lax.rem(x + k, NX), c) for k in range(NX)]


def product_z_kernel(hops, cols, where_ref, lhs_ref, rhs_ref, keep_ref, send_ref, acc):
    z, x, c = where_ref[0], where_ref[1], where_ref[2]
    s = 1 - 2 * c
    near, far = near_x(x, c), near_x(x, 1 - c)

    def put(ref, at, groups):
        for i, (gx, gc) in enumerate(groups):
            row = pl.multiple_of(gx * 64 + gc * 32, 32)
            ref[at + i] = acc[pl.ds(row, 32), :]

    at = 0
    for hop in hops:
        acc[...] = dot(lhs_ref, rhs_ref, lax.rem(z + s * hop + NZ, NZ), 0, cols)
        if hop in (0, NZ // 2):
            put(keep_ref, at, near)
            put(send_ref, at, far)
            at += 4
        else:
            put(keep_ref, at, near + far)
            acc[...] = dot(lhs_ref, rhs_ref, lax.rem(z - s * hop + NZ, NZ), 0, cols)
            put(send_ref, at, far + near)
            at += 8


def product_far_kernel(
    cols, where_ref, lhs_hbm, rhs_hbm, lhs_ref, rhs_ref, keep_ref, send_ref, acc, lhs_sems, rhs_sems
):
    z, x, c = where_ref[0], where_ref[1], where_ref[2]
    far = lax.rem(z + NZ // 2, NZ)

    def bring(hbm, ref, part, sem):
        copy = pltpu.make_async_copy(hbm.at[:, part], ref.at[:, part], sem)
        copy.start()
        return copy

    first = bring(rhs_hbm, rhs_ref, pl.ds(0, cols), rhs_sems.at[0])
    blocks = [
        bring(lhs_hbm, lhs_ref, pl.ds(pl.multiple_of(lax.rem(far + k, NZ) * 256, 256), 256), lhs_sems.at[k])
        for k in range(NZ)
    ]
    rest = bring(rhs_hbm, rhs_ref, pl.ds(cols, rhs_ref.shape[1] - cols), rhs_sems.at[1])
    first.wait()
    blocks[0].wait()
    acc[...] = dot(lhs_ref, rhs_ref, far, 0, cols)
    for ref, core in ((keep_ref, c), (send_ref, 1 - c)):
        for i, (gx, gc) in enumerate(near_x(x, core)):
            ref[i] = acc[pl.ds(pl.multiple_of(gx * 64 + gc * 32, 32), 32), :]
    for block in blocks[1:]:
        block.wait()
    rest.wait()


def product_x_kernel(start, cols, where_ref, lhs_ref, rhs_ref, keep2_ref, send2_ref, keep_ref, send_ref, acc):
    z, x, c = where_ref[0], where_ref[1], where_ref[2]
    s = 1 - 2 * c
    ahead, behind, across = lax.rem(x + s + NX, NX), lax.rem(x - s + NX, NX), lax.rem(x + 2, NX)

    def rows(gx, gc):
        return acc[pl.ds(pl.multiple_of(gx * 64 + gc * 32, 32), 32), :]

    def put(slot, group, near):
        if near:
            keep_ref[slot] = rows(ahead, group)
            send_ref[8 + slot] = rows(behind, group)
            keep2_ref[slot] = rows(across, group)
            keep_ref[16 + slot] = rows(x, group)
        else:
            keep_ref[8 + slot] = rows(ahead, group)
            send_ref[slot] = rows(behind, group)
            send2_ref[slot] = rows(across, group)
            send_ref[16 + slot] = rows(x, group)

    @pl.loop(0, NZ)
    def _(t):
        acc[...] = dot(lhs_ref, rhs_ref, lax.rem(z + s * t + NZ, NZ), start, cols)

        @pl.when(jnp.logical_and(t > 0, t < 4))
        def _():
            put(2 * t - 2, c, True)
            put(2 * t - 1, 1 - c, True)

        @pl.when(t > 4)
        def _():
            put(14 - 2 * t, 1 - c, False)
            put(15 - 2 * t, c, False)

        @pl.when(jnp.logical_or(t == 0, t == 4))
        def _():
            slot = jnp.where(t == 4, 6, 7)
            put(slot, c, True)
            put(slot, 1 - c, False)


VMEM = pl.BlockSpec(memory_space=pltpu.VMEM)


def product(kernel, groups, cols, rows, where, grad_out, attn_out):
    return pl.pallas_call(
        kernel,
        in_specs=[pl.BlockSpec(memory_space=pltpu.SMEM), VMEM, VMEM],
        out_specs=[VMEM] * len(groups),
        out_shape=[jax.ShapeDtypeStruct((g, 32, cols), jnp.float32) for g in groups],
        scratch_shapes=[pltpu.VMEM((256, cols), jnp.float32)],
        compiler_params=pltpu.CompilerParams(vmem_limit_bytes=VLIM),
        cost_estimate=pl.CostEstimate(flops=COST * rows * cols, bytes_accessed=COST * rows, transcendentals=0),
    )(where, grad_out, attn_out)


def product_far(where, grad_out, attn_out):
    hbm = pl.BlockSpec(memory_space=pltpu.HBM)
    return pl.pallas_call(
        functools.partial(product_far_kernel, COLS_Z),
        in_specs=[pl.BlockSpec(memory_space=pltpu.SMEM), hbm, hbm],
        out_specs=[VMEM] * 4,
        out_shape=[jax.ShapeDtypeStruct(v.shape, v.dtype) for v in (grad_out, attn_out)]
        + [jax.ShapeDtypeStruct((4, 32, COLS_Z), jnp.float32)] * 2,
        scratch_shapes=[
            pltpu.VMEM((256, COLS_Z), jnp.float32),
            pltpu.SemaphoreType.DMA((NZ,)),
            pltpu.SemaphoreType.DMA((2,)),
        ],
        compiler_params=pltpu.CompilerParams(vmem_limit_bytes=VFAR),
        cost_estimate=pl.CostEstimate(flops=COST * 256 * COLS_Z, bytes_accessed=COST * 256, transcendentals=0),
    )(where, grad_out, attn_out)


VFAR = 43 << 20
VLIM = 24 << 20
COST = 1


def other_core(value):
    return lax.ppermute(value, "c", [(0, 1), (1, 0)])


def onward(value, axis):
    n = SIZE[axis]
    return lax.ppermute(value, (axis, "c"), [(2 * i + c, 2 * ((i + 1 - 2 * c) % n) + c) for i in range(n) for c in range(2)])


def shift(value, axis, by):
    n = SIZE[axis]
    return lax.ppermute(value, axis, [(i, (i + by) % n) for i in range(n)])


def at_front(part, whole):
    return lax.pad(part, jnp.float32(0), [(0, whole - part.shape[0], 0), (0, 0, 0), (0, 0, 0)])


def sum_over(tile, axes, n):
    copies = jnp.broadcast_to(tile[None], (n,) + tile.shape)
    return jnp.sum(lax.all_to_all(copies, axes, 0, 0, tiled=True), axis=0)


def after(value, *others):
    return lax.optimization_barrier((value, others))[0]


def shards(attn_out, grad_out, grad_acc, master_weight, moment_m, moment_v):
    entry_count = 2048 * 8192
    where = jnp.stack([lax.axis_index(a) for a in DP]).astype(jnp.int32)

    def product_z(where, hops):
        groups = sum(4 if hop in (0, NZ // 2) else 8 for hop in hops)
        return product(
            functools.partial(product_z_kernel, hops, COLS_Z), [groups] * 2, COLS_Z, groups * 64, where, grad_out, attn_out
        )

    def both(pair):
        return pair[0] + pair[1]

    cols_x = attn_out.shape[1] - COLS_Z

    def add(here, moving):
        return here + (moving if moving.shape == here.shape else at_front(moving, here.shape[0]))

    grad_out, attn_out, keep4, send4 = product_far(where, grad_out, attn_out)
    pair4 = (keep4, other_core(send4))
    pair3 = product_z(after(where, pair4[0]), (3,))
    pair3 = (pair3[0], other_core(pair3[1]))
    first_z = lax.optimization_barrier(both(pair4))
    keep_far, send_far, keep_x, send_x = product(
        functools.partial(product_x_kernel, COLS_Z, cols_x),
        [8, 8, 24, 24], cols_x, 2048, after(where, pair3[0], first_z), grad_out, attn_out,
    )
    next_z = add(both(pair3)[:8], onward(first_z, "z"))
    far_x = (keep_far, after(other_core(send_far), next_z))
    pair2 = product_z(after(where, keep_far, next_z), (2,))
    pair2 = (pair2[0], other_core(pair2[1]))
    first_x = lax.optimization_barrier(both(far_x))
    pair_x = (keep_x, other_core(after(send_x, first_x)))
    pair1 = product_z(after(where, pair2[0], first_x), (1, 0))
    pair1 = (pair1[0], other_core(pair1[1]))

    z = onward(next_z, "z")
    for pair in (pair2, pair1):
        z = onward(add(both(pair)[:8], z), "z")
    x = onward(first_x, "x")
    x = onward(add(both(pair_x)[:16], x), "x")
    sum_x = x[:8] + other_core(x[8:]) + both(pair_x)[16:24]

    moving = onward(sum_x[6:7], "z")
    z = after(z, moving)
    moving = add(sum_x[4:6], after(moving, z))
    sum_z = z[:4] + other_core(after(z[4:], moving)) + both(pair1)[8:12]
    batch_z = sum_z[0] + sum(shift(sum_z[k], "x", k) for k in (1, 2, 3))
    moving = onward(moving, "z")
    moving = onward(sum_x[2:4] + moving, "z")
    moving = onward(sum_x[0:2] + after(moving, batch_z), "z")
    batch_x = moving[0] + other_core(moving[1]) + sum_x[7]
    gradient = grad_acc + jnp.concatenate([batch_z, batch_x], axis=1)

    energy = jnp.sum((gradient * gradient).reshape(4, 8, 16, 128), axis=(0, 2))
    energy = sum_over(sum_over(energy, ("z", "c"), 16), ("x", "y"), 16)
    divisor = jnp.sqrt(jnp.sum(energy) / entry_count + epsilon)
    clipped = gradient / divisor
    moment_new = beta_first * moment_m + (1.0 - beta_first) * clipped
    second_new = beta_second * moment_v + (1.0 - beta_second) * clipped * clipped
    update = moment_new / (jnp.sqrt(second_new) + epsilon) + weight_decay * master_weight
    squares = jnp.stack([jnp.sum(master_weight * master_weight, axis=1), jnp.sum(update * update, axis=1)])
    norms = jnp.sqrt(lax.psum(squares, "y"))
    trust = norms[0] / (norms[1] + epsilon)
    return moment_new, second_new, trust[:, None] * update


def solution(mesh):
    fine = Mesh(mesh.devices.reshape(NZ, NX, 2, 4), DP + ("y",))
    split = P(DP, "y")
    return jax.shard_map(
        shards, mesh=fine, in_specs=(split, P(DP, None)) + (split,) * 4, out_specs=(split,) * 3, check_vma=False
    )
```

```python
import functools

import jax
import jax.numpy as jnp
from jax import lax
from jax.experimental import pallas as pl
from jax.experimental.pallas import tpu as pltpu
from jax.sharding import Mesh, PartitionSpec as P

beta_first = 0.9
beta_second = 0.999
weight_decay = 0.01
epsilon = 1e-06

DP = ("z", "x", "c")
NZ, NX = 8, 4
SIZE = {"z": NZ, "x": NX}
COLS_Z = 1152


def dot(lhs_ref, rhs_ref, z, start, cols):
    lhs = lhs_ref[:, pl.ds(pl.multiple_of(z * 256, 256), 256)]
    rhs = rhs_ref[:, start : start + cols]
    return lax.dot_general(lhs, rhs, (((0,), (0,)), ((), ())), preferred_element_type=jnp.float32)


def near_x(x, c):
    return [(lax.rem(x + k, NX), c) for k in range(NX)]


def product_z_kernel(hops, cols, where_ref, lhs_ref, rhs_ref, keep_ref, send_ref, acc):
    z, x, c = where_ref[0], where_ref[1], where_ref[2]
    s = 1 - 2 * c
    near, far = near_x(x, c), near_x(x, 1 - c)

    def put(ref, at, groups):
        for i, (gx, gc) in enumerate(groups):
            row = pl.multiple_of(gx * 64 + gc * 32, 32)
            ref[at + i] = acc[pl.ds(row, 32), :]

    at = 0
    for hop in hops:
        acc[...] = dot(lhs_ref, rhs_ref, lax.rem(z + s * hop + NZ, NZ), 0, cols)
        if hop in (0, NZ // 2):
            put(keep_ref, at, near)
            put(send_ref, at, far)
            at += 4
        else:
            put(keep_ref, at, near + far)
            acc[...] = dot(lhs_ref, rhs_ref, lax.rem(z - s * hop + NZ, NZ), 0, cols)
            put(send_ref, at, far + near)
            at += 8


def product_far_kernel(
    cols, where_ref, lhs_hbm, rhs_hbm, lhs_ref, rhs_ref, keep_ref, send_ref, acc, lhs_sems, rhs_sems
):
    z, x, c = where_ref[0], where_ref[1], where_ref[2]
    far = lax.rem(z + NZ // 2, NZ)

    def bring(hbm, ref, part, sem):
        copy = pltpu.make_async_copy(hbm.at[:, part], ref.at[:, part], sem)
        copy.start()
        return copy

    first = bring(rhs_hbm, rhs_ref, pl.ds(0, cols), rhs_sems.at[0])
    blocks = [
        bring(lhs_hbm, lhs_ref, pl.ds(pl.multiple_of(lax.rem(far + k, NZ) * 256, 256), 256), lhs_sems.at[k])
        for k in range(NZ)
    ]
    rest = bring(rhs_hbm, rhs_ref, pl.ds(cols, rhs_ref.shape[1] - cols), rhs_sems.at[1])
    first.wait()
    blocks[0].wait()
    acc[...] = dot(lhs_ref, rhs_ref, far, 0, cols)
    for ref, core in ((keep_ref, c), (send_ref, 1 - c)):
        for i, (gx, gc) in enumerate(near_x(x, core)):
            ref[i] = acc[pl.ds(pl.multiple_of(gx * 64 + gc * 32, 32), 32), :]
    for block in blocks[1:]:
        block.wait()
    rest.wait()


def product_x_kernel(start, cols, where_ref, lhs_ref, rhs_ref, keep2_ref, send2_ref, keep_ref, send_ref, acc):
    z, x, c = where_ref[0], where_ref[1], where_ref[2]
    s = 1 - 2 * c
    ahead, behind, across = lax.rem(x + s + NX, NX), lax.rem(x - s + NX, NX), lax.rem(x + 2, NX)

    def rows(gx, gc):
        return acc[pl.ds(pl.multiple_of(gx * 64 + gc * 32, 32), 32), :]

    def put(slot, group, near):
        if near:
            keep_ref[slot] = rows(ahead, group)
            send_ref[8 + slot] = rows(behind, group)
            keep2_ref[slot] = rows(across, group)
            keep_ref[16 + slot] = rows(x, group)
        else:
            keep_ref[8 + slot] = rows(ahead, group)
            send_ref[slot] = rows(behind, group)
            send2_ref[slot] = rows(across, group)
            send_ref[16 + slot] = rows(x, group)

    @pl.loop(0, NZ)
    def _(t):
        acc[...] = dot(lhs_ref, rhs_ref, lax.rem(z + s * t + NZ, NZ), start, cols)

        @pl.when(jnp.logical_and(t > 0, t < 4))
        def _():
            put(2 * t - 2, c, True)
            put(2 * t - 1, 1 - c, True)

        @pl.when(t > 4)
        def _():
            put(14 - 2 * t, 1 - c, False)
            put(15 - 2 * t, c, False)

        @pl.when(jnp.logical_or(t == 0, t == 4))
        def _():
            slot = jnp.where(t == 4, 6, 7)
            put(slot, c, True)
            put(slot, 1 - c, False)


VMEM = pl.BlockSpec(memory_space=pltpu.VMEM)


def product(kernel, groups, cols, rows, where, grad_out, attn_out):
    return pl.pallas_call(
        kernel,
        in_specs=[pl.BlockSpec(memory_space=pltpu.SMEM), VMEM, VMEM],
        out_specs=[VMEM] * len(groups),
        out_shape=[jax.ShapeDtypeStruct((g, 32, cols), jnp.float32) for g in groups],
        scratch_shapes=[pltpu.VMEM((256, cols), jnp.float32)],
        compiler_params=pltpu.CompilerParams(vmem_limit_bytes=VLIM),
        cost_estimate=pl.CostEstimate(flops=COST * rows * cols, bytes_accessed=COST * rows, transcendentals=0),
    )(where, grad_out, attn_out)


def product_far(where, grad_out, attn_out):
    hbm = pl.BlockSpec(memory_space=pltpu.HBM)
    return pl.pallas_call(
        functools.partial(product_far_kernel, COLS_Z),
        in_specs=[pl.BlockSpec(memory_space=pltpu.SMEM), hbm, hbm],
        out_specs=[VMEM] * 4,
        out_shape=[jax.ShapeDtypeStruct(v.shape, v.dtype) for v in (grad_out, attn_out)]
        + [jax.ShapeDtypeStruct((4, 32, COLS_Z), jnp.float32)] * 2,
        scratch_shapes=[
            pltpu.VMEM((256, COLS_Z), jnp.float32),
            pltpu.SemaphoreType.DMA((NZ,)),
            pltpu.SemaphoreType.DMA((2,)),
        ],
        compiler_params=pltpu.CompilerParams(vmem_limit_bytes=VFAR),
        cost_estimate=pl.CostEstimate(flops=COST * 256 * COLS_Z, bytes_accessed=COST * 256, transcendentals=0),
    )(where, grad_out, attn_out)


VFAR = 43 << 20
VLIM = 24 << 20
COST = 1


def other_core(value):
    return lax.ppermute(value, "c", [(0, 1), (1, 0)])


def onward(value, axis):
    n = SIZE[axis]
    return lax.ppermute(value, (axis, "c"), [(2 * i + c, 2 * ((i + 1 - 2 * c) % n) + c) for i in range(n) for c in range(2)])


def shift(value, axis, by):
    n = SIZE[axis]
    return lax.ppermute(value, axis, [(i, (i + by) % n) for i in range(n)])


def at_front(part, whole):
    return lax.pad(part, jnp.float32(0), [(0, whole - part.shape[0], 0), (0, 0, 0), (0, 0, 0)])


def sum_over(tile, axes, n):
    copies = jnp.broadcast_to(tile[None], (n,) + tile.shape)
    return jnp.sum(lax.all_to_all(copies, axes, 0, 0, tiled=True), axis=0)


def after(value, *others):
    return lax.optimization_barrier((value, others))[0]


def shards(attn_out, grad_out, grad_acc, master_weight, moment_m, moment_v):
    entry_count = 2048 * 8192
    where = jnp.stack([lax.axis_index(a) for a in DP]).astype(jnp.int32)

    def product_z(where, hops):
        groups = sum(4 if hop in (0, NZ // 2) else 8 for hop in hops)
        return product(
            functools.partial(product_z_kernel, hops, COLS_Z), [groups] * 2, COLS_Z, groups * 64, where, grad_out, attn_out
        )

    def both(pair):
        return pair[0] + pair[1]

    cols_x = attn_out.shape[1] - COLS_Z

    def add(here, moving):
        return here + (moving if moving.shape == here.shape else at_front(moving, here.shape[0]))

    cuts = (slice(0, 640), slice(640, COLS_Z))

    def hop_z(pair, parts):
        ahead = add(both(pair)[:8, :, cuts[0]], parts[0])
        return ahead, add(both(pair)[:8, :, cuts[1]], after(parts[1], ahead))

    grad_out, attn_out, keep4, send4 = product_far(where, grad_out, attn_out)
    pair4 = (keep4, other_core(send4))
    pair3 = product_z(after(where, pair4[0]), (3,))
    pair3 = (pair3[0], other_core(pair3[1]))
    first_z = lax.optimization_barrier(both(pair4))
    keep_far, send_far, keep_x, send_x = product(
        functools.partial(product_x_kernel, COLS_Z, cols_x),
        [8, 8, 24, 24], cols_x, 2048, after(where, pair3[0], first_z), grad_out, attn_out,
    )
    pair2 = product_z(after(where, keep_far), (2,))
    next_z = add(both(pair3)[:8], after(onward(first_z, "z"), pair2[0]))
    far_x = (keep_far, after(other_core(send_far), next_z))
    pair2 = (pair2[0], other_core(pair2[1]))
    first_x = lax.optimization_barrier(both(far_x))
    pair_x = (keep_x, other_core(after(send_x, first_x)))
    pair1 = product_z(after(where, pair2[0], first_x), (1, 0))
    pair1 = (pair1[0], other_core(pair1[1]))

    next_z = onward(next_z, "z")
    z = [next_z[..., cut] for cut in cuts]
    for pair in (pair2, pair1):
        steps = hop_z(pair, z)
        z = [onward(part, "z") for part in steps]
    x = after(onward(first_x, "x"), pair1[0])
    x = after(onward(add(both(pair_x)[:16], x), "x"), z[0], steps[1])
    sum_x = x[:8] + other_core(x[8:]) + both(pair_x)[16:24]

    moving = onward(sum_x[6:7], "z")
    far = [other_core(z[0][4:])]
    z[1] = after(z[1], moving)
    moving = add(sum_x[4:6], after(moving, z[1]))
    far.append(other_core(after(z[1][4:], moving)))
    sum_z = jnp.concatenate([z[i][:4] + far[i] for i in range(2)], axis=2) + both(pair1)[8:12]
    batch_z = sum_z[0] + sum(shift(sum_z[k], "x", k) for k in (1, 2, 3))
    moving = onward(moving, "z")
    moving = onward(sum_x[2:4] + moving, "z")
    moving = onward(sum_x[0:2] + after(moving, batch_z), "z")
    batch_x = moving[0] + other_core(moving[1]) + sum_x[7]
    gradient = grad_acc + jnp.concatenate([batch_z, batch_x], axis=1)

    energy = jnp.sum((gradient * gradient).reshape(4, 8, 16, 128), axis=(0, 2))
    energy = sum_over(sum_over(energy, ("z", "c"), 16), ("x", "y"), 16)
    divisor = jnp.sqrt(jnp.sum(energy) / entry_count + epsilon)
    clipped = gradient / divisor
    moment_new = beta_first * moment_m + (1.0 - beta_first) * clipped
    second_new = beta_second * moment_v + (1.0 - beta_second) * clipped * clipped
    update = moment_new / (jnp.sqrt(second_new) + epsilon) + weight_decay * master_weight
    squares = jnp.stack([jnp.sum(master_weight * master_weight, axis=1), jnp.sum(update * update, axis=1)])
    norms = jnp.sqrt(lax.psum(squares, "y"))
    trust = norms[0] / (norms[1] + epsilon)
    return moment_new, second_new, trust[:, None] * update


def solution(mesh):
    fine = Mesh(mesh.devices.reshape(NZ, NX, 2, 4), DP + ("y",))
    split = P(DP, "y")
    return jax.shard_map(
        shards, mesh=fine, in_specs=(split, P(DP, None)) + (split,) * 4, out_specs=(split,) * 3, check_vma=False
    )
```

```python
import functools

import jax
import jax.numpy as jnp
from jax import lax
from jax.experimental import pallas as pl
from jax.experimental.pallas import tpu as pltpu
from jax.sharding import Mesh, PartitionSpec as P

beta_first = 0.9
beta_second = 0.999
weight_decay = 0.01
epsilon = 1e-06

DP = ("z", "x", "c")
NZ, NX = 8, 4
SIZE = {"z": NZ, "x": NX}
COLS_Z = 1280


def dot(lhs_ref, rhs_ref, z, start, cols):
    lhs = lhs_ref[:, pl.ds(pl.multiple_of(z * 256, 256), 256)]
    rhs = rhs_ref[:, start : start + cols]
    return lax.dot_general(lhs, rhs, (((0,), (0,)), ((), ())), preferred_element_type=jnp.float32)


def near_x(x, c):
    return [(lax.rem(x + k, NX), c) for k in range(NX)]


def product_z_kernel(hops, cols, where_ref, lhs_ref, rhs_ref, keep_ref, send_ref, acc):
    z, x, c = where_ref[0], where_ref[1], where_ref[2]
    s = 1 - 2 * c
    near, far = near_x(x, c), near_x(x, 1 - c)

    def put(ref, at, groups):
        for i, (gx, gc) in enumerate(groups):
            row = pl.multiple_of(gx * 64 + gc * 32, 32)
            ref[at + i] = acc[pl.ds(row, 32), :]

    at = 0
    for hop in hops:
        acc[...] = dot(lhs_ref, rhs_ref, lax.rem(z + s * hop + NZ, NZ), 0, cols)
        if hop in (0, NZ // 2):
            put(keep_ref, at, near)
            put(send_ref, at, far)
            at += 4
        else:
            put(keep_ref, at, near + far)
            acc[...] = dot(lhs_ref, rhs_ref, lax.rem(z - s * hop + NZ, NZ), 0, cols)
            put(send_ref, at, far + near)
            at += 8


def product_far_kernel(
    cols, where_ref, lhs_hbm, rhs_hbm, lhs_ref, rhs_ref, keep_ref, send_ref, acc, lhs_sems, rhs_sems
):
    z, x, c = where_ref[0], where_ref[1], where_ref[2]
    far = lax.rem(z + NZ // 2, NZ)

    def bring(hbm, ref, part, sem):
        copy = pltpu.make_async_copy(hbm.at[:, part], ref.at[:, part], sem)
        copy.start()
        return copy

    first = bring(rhs_hbm, rhs_ref, pl.ds(0, cols), rhs_sems.at[0])
    blocks = [
        bring(lhs_hbm, lhs_ref, pl.ds(pl.multiple_of(lax.rem(far + k, NZ) * 256, 256), 256), lhs_sems.at[k])
        for k in range(NZ)
    ]
    rest = bring(rhs_hbm, rhs_ref, pl.ds(cols, rhs_ref.shape[1] - cols), rhs_sems.at[1])
    first.wait()
    blocks[0].wait()
    acc[...] = dot(lhs_ref, rhs_ref, far, 0, cols)
    for ref, core in ((keep_ref, c), (send_ref, 1 - c)):
        for i, (gx, gc) in enumerate(near_x(x, core)):
            ref[i] = acc[pl.ds(pl.multiple_of(gx * 64 + gc * 32, 32), 32), :]
    for block in blocks[1:]:
        block.wait()
    rest.wait()


def product_x_kernel(start, cols, where_ref, lhs_ref, rhs_ref, keep2_ref, send2_ref, keep_ref, send_ref, acc):
    z, x, c = where_ref[0], where_ref[1], where_ref[2]
    s = 1 - 2 * c
    ahead, behind, across = lax.rem(x + s + NX, NX), lax.rem(x - s + NX, NX), lax.rem(x + 2, NX)

    def rows(gx, gc):
        return acc[pl.ds(pl.multiple_of(gx * 64 + gc * 32, 32), 32), :]

    def put(slot, group, near):
        if near:
            keep_ref[slot] = rows(ahead, group)
            send_ref[8 + slot] = rows(behind, group)
            keep2_ref[slot] = rows(across, group)
            keep_ref[16 + slot] = rows(x, group)
        else:
            keep_ref[8 + slot] = rows(ahead, group)
            send_ref[slot] = rows(behind, group)
            send2_ref[slot] = rows(across, group)
            send_ref[16 + slot] = rows(x, group)

    @pl.loop(0, NZ)
    def _(t):
        acc[...] = dot(lhs_ref, rhs_ref, lax.rem(z + s * t + NZ, NZ), start, cols)

        @pl.when(jnp.logical_and(t > 0, t < 4))
        def _():
            put(2 * t - 2, c, True)
            put(2 * t - 1, 1 - c, True)

        @pl.when(t > 4)
        def _():
            put(14 - 2 * t, 1 - c, False)
            put(15 - 2 * t, c, False)

        @pl.when(jnp.logical_or(t == 0, t == 4))
        def _():
            slot = jnp.where(t == 4, 6, 7)
            put(slot, c, True)
            put(slot, 1 - c, False)


VMEM = pl.BlockSpec(memory_space=pltpu.VMEM)


def product(kernel, groups, cols, rows, where, grad_out, attn_out):
    return pl.pallas_call(
        kernel,
        in_specs=[pl.BlockSpec(memory_space=pltpu.SMEM), VMEM, VMEM],
        out_specs=[VMEM] * len(groups),
        out_shape=[jax.ShapeDtypeStruct((g, 32, cols), jnp.float32) for g in groups],
        scratch_shapes=[pltpu.VMEM((256, cols), jnp.float32)],
        compiler_params=pltpu.CompilerParams(vmem_limit_bytes=VLIM),
        cost_estimate=pl.CostEstimate(flops=COST * rows * cols, bytes_accessed=COST * rows, transcendentals=0),
    )(where, grad_out, attn_out)


def product_far(where, grad_out, attn_out):
    hbm = pl.BlockSpec(memory_space=pltpu.HBM)
    return pl.pallas_call(
        functools.partial(product_far_kernel, COLS_Z),
        in_specs=[pl.BlockSpec(memory_space=pltpu.SMEM), hbm, hbm],
        out_specs=[VMEM] * 4,
        out_shape=[jax.ShapeDtypeStruct(v.shape, v.dtype) for v in (grad_out, attn_out)]
        + [jax.ShapeDtypeStruct((4, 32, COLS_Z), jnp.float32)] * 2,
        scratch_shapes=[
            pltpu.VMEM((256, COLS_Z), jnp.float32),
            pltpu.SemaphoreType.DMA((NZ,)),
            pltpu.SemaphoreType.DMA((2,)),
        ],
        compiler_params=pltpu.CompilerParams(vmem_limit_bytes=VFAR),
        cost_estimate=pl.CostEstimate(flops=COST * 256 * COLS_Z, bytes_accessed=COST * 256, transcendentals=0),
    )(where, grad_out, attn_out)


VFAR = 43 << 20
VLIM = 24 << 20
COST = 1


def other_core(value):
    return lax.ppermute(value, "c", [(0, 1), (1, 0)])


def onward(value, axis):
    n = SIZE[axis]
    return lax.ppermute(value, (axis, "c"), [(2 * i + c, 2 * ((i + 1 - 2 * c) % n) + c) for i in range(n) for c in range(2)])


def shift(value, axis, by):
    n = SIZE[axis]
    return lax.ppermute(value, axis, [(i, (i + by) % n) for i in range(n)])


def at_front(part, whole):
    return lax.pad(part, jnp.float32(0), [(0, whole - part.shape[0], 0), (0, 0, 0), (0, 0, 0)])


def sum_over(tile, axes, n):
    copies = jnp.broadcast_to(tile[None], (n,) + tile.shape)
    return jnp.sum(lax.all_to_all(copies, axes, 0, 0, tiled=True), axis=0)


def after(value, *others):
    return lax.optimization_barrier((value, others))[0]


def shards(attn_out, grad_out, grad_acc, master_weight, moment_m, moment_v):
    entry_count = 2048 * 8192
    where = jnp.stack([lax.axis_index(a) for a in DP]).astype(jnp.int32)

    def product_z(where, hops):
        groups = sum(4 if hop in (0, NZ // 2) else 8 for hop in hops)
        return product(
            functools.partial(product_z_kernel, hops, COLS_Z), [groups] * 2, COLS_Z, groups * 64, where, grad_out, attn_out
        )

    def both(pair):
        return pair[0] + pair[1]

    cols_x = attn_out.shape[1] - COLS_Z

    def add(here, moving):
        return here + (moving if moving.shape == here.shape else at_front(moving, here.shape[0]))

    cuts = (slice(0, 640), slice(640, COLS_Z))

    def hop_z(pair, parts):
        ahead = add(both(pair)[:8, :, cuts[0]], parts[0])
        return ahead, add(both(pair)[:8, :, cuts[1]], after(parts[1], ahead))

    grad_out, attn_out, keep4, send4 = product_far(where, grad_out, attn_out)
    pair4 = (keep4, other_core(send4))
    pair3 = product_z(after(where, pair4[0]), (3,))
    pair3 = (pair3[0], other_core(pair3[1]))
    first_z = lax.optimization_barrier(both(pair4))
    keep_far, send_far, keep_x, send_x = product(
        functools.partial(product_x_kernel, COLS_Z, cols_x),
        [8, 8, 24, 24], cols_x, 2048, after(where, pair3[0], first_z), grad_out, attn_out,
    )
    pair2 = product_z(after(where, keep_far), (2,))
    next_z = add(both(pair3)[:8], after(onward(first_z, "z"), pair2[0]))
    far_x = (keep_far, after(other_core(send_far), next_z))
    pair2 = (pair2[0], other_core(pair2[1]))
    first_x = lax.optimization_barrier(both(far_x))
    pair_x = (keep_x, other_core(after(send_x, first_x)))
    pair1 = product_z(after(where, pair2[0], first_x), (1, 0))
    pair1 = (pair1[0], other_core(pair1[1]))

    next_z = onward(next_z, "z")
    z = [next_z[..., cut] for cut in cuts]
    steps = []
    for pair in (pair2, pair1):
        steps.append(hop_z(pair, z))
        z = [onward(part, "z") for part in steps[-1]]
    x = after(onward(first_x, "x"), pair1[0])
    x = after(onward(add(both(pair_x)[:16], x), "x"), steps[0][1])
    sum_x = x[:8] + other_core(x[8:]) + both(pair_x)[16:24]

    moving = onward(sum_x[6:7], "z")
    far = [other_core(z[0][4:])]
    z[1] = after(z[1], moving)
    moving = add(sum_x[4:6], after(moving, z[1]))
    far.append(other_core(after(z[1][4:], moving)))
    sum_z = jnp.concatenate([z[i][:4] + far[i] for i in range(2)], axis=2) + both(pair1)[8:12]
    batch_z = sum_z[0] + sum(shift(sum_z[k], "x", k) for k in (1, 2, 3))
    moving = onward(moving, "z")
    moving = onward(sum_x[2:4] + moving, "z")
    moving = onward(sum_x[0:2] + after(moving, batch_z), "z")
    batch_x = moving[0] + other_core(moving[1]) + sum_x[7]
    gradient = grad_acc + jnp.concatenate([batch_z, batch_x], axis=1)

    energy = jnp.sum((gradient * gradient).reshape(4, 8, 16, 128), axis=(0, 2))
    energy = sum_over(sum_over(energy, ("z", "c"), 16), ("x", "y"), 16)
    divisor = jnp.sqrt(jnp.sum(energy) / entry_count + epsilon)
    clipped = gradient / divisor
    moment_new = beta_first * moment_m + (1.0 - beta_first) * clipped
    second_new = beta_second * moment_v + (1.0 - beta_second) * clipped * clipped
    update = moment_new / (jnp.sqrt(second_new) + epsilon) + weight_decay * master_weight
    squares = jnp.stack([jnp.sum(master_weight * master_weight, axis=1), jnp.sum(update * update, axis=1)])
    norms = jnp.sqrt(lax.psum(squares, "y"))
    trust = norms[0] / (norms[1] + epsilon)
    return moment_new, second_new, trust[:, None] * update


def solution(mesh):
    fine = Mesh(mesh.devices.reshape(NZ, NX, 2, 4), DP + ("y",))
    split = P(DP, "y")
    return jax.shard_map(
        shards, mesh=fine, in_specs=(split, P(DP, None)) + (split,) * 4, out_specs=(split,) * 3, check_vma=False
    )
```

```python
import functools

import jax
import jax.numpy as jnp
from jax import lax
from jax.experimental import pallas as pl
from jax.experimental.pallas import tpu as pltpu
from jax.sharding import Mesh, PartitionSpec as P

beta_first = 0.9
beta_second = 0.999
weight_decay = 0.01
epsilon = 1e-06

DP = ("z", "x", "c")
NZ, NX = 8, 4
SIZE = {"z": NZ, "x": NX}
COLS_Z = 1280


def dot(lhs_ref, rhs_ref, z, start, cols):
    lhs = lhs_ref[:, pl.ds(pl.multiple_of(z * 256, 256), 256)]
    rhs = rhs_ref[:, start : start + cols]
    return lax.dot_general(lhs, rhs, (((0,), (0,)), ((), ())), preferred_element_type=jnp.float32)


def near_x(x, c):
    return [(lax.rem(x + k, NX), c) for k in range(NX)]


def product_z_kernel(hops, cols, where_ref, lhs_ref, rhs_ref, keep_ref, send_ref, acc):
    z, x, c = where_ref[0], where_ref[1], where_ref[2]
    s = 1 - 2 * c
    near, far = near_x(x, c), near_x(x, 1 - c)

    def put(ref, at, groups):
        for i, (gx, gc) in enumerate(groups):
            row = pl.multiple_of(gx * 64 + gc * 32, 32)
            ref[at + i] = acc[pl.ds(row, 32), :]

    at = 0
    for hop in hops:
        acc[...] = dot(lhs_ref, rhs_ref, lax.rem(z + s * hop + NZ, NZ), 0, cols)
        if hop in (0, NZ // 2):
            put(keep_ref, at, near)
            put(send_ref, at, far)
            at += 4
        else:
            put(keep_ref, at, near + far)
            acc[...] = dot(lhs_ref, rhs_ref, lax.rem(z - s * hop + NZ, NZ), 0, cols)
            put(send_ref, at, far + near)
            at += 8


def product_far_kernel(
    cols, where_ref, lhs_hbm, rhs_hbm, lhs_ref, rhs_ref, keep_ref, send_ref, acc, lhs_sems, rhs_sems
):
    z, x, c = where_ref[0], where_ref[1], where_ref[2]
    far = lax.rem(z + NZ // 2, NZ)

    def bring(hbm, ref, part, sem):
        copy = pltpu.make_async_copy(hbm.at[:, part], ref.at[:, part], sem)
        copy.start()
        return copy

    first = bring(rhs_hbm, rhs_ref, pl.ds(0, cols), rhs_sems.at[0])
    blocks = [
        bring(lhs_hbm, lhs_ref, pl.ds(pl.multiple_of(lax.rem(far + k, NZ) * 256, 256), 256), lhs_sems.at[k])
        for k in range(NZ)
    ]
    rest = bring(rhs_hbm, rhs_ref, pl.ds(cols, rhs_ref.shape[1] - cols), rhs_sems.at[1])
    first.wait()
    blocks[0].wait()
    acc[...] = dot(lhs_ref, rhs_ref, far, 0, cols)
    for ref, core in ((keep_ref, c), (send_ref, 1 - c)):
        for i, (gx, gc) in enumerate(near_x(x, core)):
            ref[i] = acc[pl.ds(pl.multiple_of(gx * 64 + gc * 32, 32), 32), :]
    for block in blocks[1:]:
        block.wait()
    rest.wait()


def product_x_kernel(start, cols, where_ref, lhs_ref, rhs_ref, keep2_ref, send2_ref, keep_ref, send_ref, acc):
    z, x, c = where_ref[0], where_ref[1], where_ref[2]
    s = 1 - 2 * c
    ahead, behind, across = lax.rem(x + s + NX, NX), lax.rem(x - s + NX, NX), lax.rem(x + 2, NX)

    def rows(gx, gc):
        return acc[pl.ds(pl.multiple_of(gx * 64 + gc * 32, 32), 32), :]

    def put(slot, group, near):
        if near:
            keep_ref[slot] = rows(ahead, group)
            send_ref[8 + slot] = rows(behind, group)
            keep2_ref[slot] = rows(across, group)
            keep_ref[16 + slot] = rows(x, group)
        else:
            keep_ref[8 + slot] = rows(ahead, group)
            send_ref[slot] = rows(behind, group)
            send2_ref[slot] = rows(across, group)
            send_ref[16 + slot] = rows(x, group)

    @pl.loop(0, NZ)
    def _(t):
        acc[...] = dot(lhs_ref, rhs_ref, lax.rem(z + s * t + NZ, NZ), start, cols)

        @pl.when(jnp.logical_and(t > 0, t < 4))
        def _():
            put(2 * t - 2, c, True)
            put(2 * t - 1, 1 - c, True)

        @pl.when(t > 4)
        def _():
            put(14 - 2 * t, 1 - c, False)
            put(15 - 2 * t, c, False)

        @pl.when(jnp.logical_or(t == 0, t == 4))
        def _():
            slot = jnp.where(t == 4, 6, 7)
            put(slot, c, True)
            put(slot, 1 - c, False)


VMEM = pl.BlockSpec(memory_space=pltpu.VMEM)


def product(kernel, groups, cols, rows, where, grad_out, attn_out):
    return pl.pallas_call(
        kernel,
        in_specs=[pl.BlockSpec(memory_space=pltpu.SMEM), VMEM, VMEM],
        out_specs=[VMEM] * len(groups),
        out_shape=[jax.ShapeDtypeStruct((g, 32, cols), jnp.float32) for g in groups],
        scratch_shapes=[pltpu.VMEM((256, cols), jnp.float32)],
        compiler_params=pltpu.CompilerParams(vmem_limit_bytes=VLIM),
        cost_estimate=pl.CostEstimate(flops=COST * rows * cols, bytes_accessed=COST * rows, transcendentals=0),
    )(where, grad_out, attn_out)


def product_far(where, grad_out, attn_out):
    hbm = pl.BlockSpec(memory_space=pltpu.HBM)
    return pl.pallas_call(
        functools.partial(product_far_kernel, COLS_Z),
        in_specs=[pl.BlockSpec(memory_space=pltpu.SMEM), hbm, hbm],
        out_specs=[VMEM] * 4,
        out_shape=[jax.ShapeDtypeStruct(v.shape, v.dtype) for v in (grad_out, attn_out)]
        + [jax.ShapeDtypeStruct((4, 32, COLS_Z), jnp.float32)] * 2,
        scratch_shapes=[
            pltpu.VMEM((256, COLS_Z), jnp.float32),
            pltpu.SemaphoreType.DMA((NZ,)),
            pltpu.SemaphoreType.DMA((2,)),
        ],
        compiler_params=pltpu.CompilerParams(vmem_limit_bytes=VFAR),
        cost_estimate=pl.CostEstimate(flops=COST * 256 * COLS_Z, bytes_accessed=COST * 256, transcendentals=0),
    )(where, grad_out, attn_out)


VFAR = 43 << 20
VLIM = 24 << 20
COST = 1


def other_core(value):
    return lax.ppermute(value, "c", [(0, 1), (1, 0)])


def onward(value, axis):
    n = SIZE[axis]
    return lax.ppermute(value, (axis, "c"), [(2 * i + c, 2 * ((i + 1 - 2 * c) % n) + c) for i in range(n) for c in range(2)])


def shift(value, axis, by):
    n = SIZE[axis]
    return lax.ppermute(value, axis, [(i, (i + by) % n) for i in range(n)])


def onward_apart(value, axis):
    n, half = SIZE[axis], value.shape[0] // 2
    cross = [(2 * i + c, 2 * ((i + 1 - 2 * c) % n) + 1 - c) for i in range(n) for c in range(2)]
    return onward(value[:half], axis) + lax.ppermute(value[half:], (axis, "c"), cross)


def at_front(part, whole):
    return lax.pad(part, jnp.float32(0), [(0, whole - part.shape[0], 0), (0, 0, 0), (0, 0, 0)])


def sum_over(tile, axes, n):
    copies = jnp.broadcast_to(tile[None], (n,) + tile.shape)
    return jnp.sum(lax.all_to_all(copies, axes, 0, 0, tiled=True), axis=0)


def after(value, *others):
    return lax.optimization_barrier((value, others))[0]


def shards(attn_out, grad_out, grad_acc, master_weight, moment_m, moment_v):
    entry_count = 2048 * 8192
    where = jnp.stack([lax.axis_index(a) for a in DP]).astype(jnp.int32)

    def product_z(where, hops):
        groups = sum(4 if hop in (0, NZ // 2) else 8 for hop in hops)
        return product(
            functools.partial(product_z_kernel, hops, COLS_Z), [groups] * 2, COLS_Z, groups * 64, where, grad_out, attn_out
        )

    def both(pair):
        return pair[0] + pair[1]

    cols_x = attn_out.shape[1] - COLS_Z

    def add(here, moving):
        return here + (moving if moving.shape == here.shape else at_front(moving, here.shape[0]))

    cuts = (slice(0, 640), slice(640, COLS_Z))

    def hop_z(pair, parts):
        ahead = add(both(pair)[:8, :, cuts[0]], parts[0])
        return ahead, add(both(pair)[:8, :, cuts[1]], after(parts[1], ahead))

    grad_out, attn_out, keep4, send4 = product_far(where, grad_out, attn_out)
    pair4 = (keep4, other_core(send4))
    pair3 = product_z(after(where, pair4[0]), (3,))
    pair3 = (pair3[0], other_core(pair3[1]))
    first_z = lax.optimization_barrier(both(pair4))
    keep_far, send_far, keep_x, send_x = product(
        functools.partial(product_x_kernel, COLS_Z, cols_x),
        [8, 8, 24, 24], cols_x, 2048, after(where, pair3[0], first_z), grad_out, attn_out,
    )
    pair2 = product_z(after(where, keep_far), (2,))
    next_z = add(both(pair3)[:8], after(onward(first_z, "z"), pair2[0]))
    far_x = (keep_far, after(other_core(send_far), next_z))
    pair2 = (pair2[0], other_core(pair2[1]))
    first_x = lax.optimization_barrier(both(far_x))
    pair_x = (keep_x, other_core(after(send_x, first_x)))
    pair1 = product_z(after(where, pair2[0], first_x), (1, 0))
    pair1 = (pair1[0], other_core(pair1[1]))

    next_z = onward(next_z, "z")
    z = [next_z[..., cut] for cut in cuts]
    steps = []
    for pair in (pair2, pair1):
        steps.append(hop_z(pair, z))
        z = [onward(part, "z") for part in steps[-1]]
    x = after(onward(first_x, "x"), pair1[0])
    x = after(onward(add(both(pair_x)[:16], x), "x"), steps[0][1])
    sum_x = x[:8] + other_core(x[8:]) + both(pair_x)[16:24]

    moving = onward(sum_x[6:7], "z")
    far = [other_core(z[0][4:])]
    z[1] = after(z[1], moving)
    moving = add(sum_x[4:6], after(moving, z[1]))
    far.append(other_core(after(z[1][4:], moving)))
    sum_z = jnp.concatenate([z[i][:4] + far[i] for i in range(2)], axis=2) + both(pair1)[8:12]
    batch_z = sum_z[0] + sum(shift(sum_z[k], "x", k) for k in (1, 2, 3))
    moving = onward(moving, "z")
    moving = onward(sum_x[2:4] + moving, "z")
    batch_x = onward_apart(sum_x[0:2] + after(moving, batch_z), "z")[0] + sum_x[7]
    gradient = grad_acc + jnp.concatenate([batch_z, batch_x], axis=1)

    energy = jnp.sum((gradient * gradient).reshape(4, 8, 16, 128), axis=(0, 2))
    energy = sum_over(sum_over(energy, ("z", "c"), 16), ("x", "y"), 16)
    divisor = jnp.sqrt(jnp.sum(energy) / entry_count + epsilon)
    clipped = gradient / divisor
    moment_new = beta_first * moment_m + (1.0 - beta_first) * clipped
    second_new = beta_second * moment_v + (1.0 - beta_second) * clipped * clipped
    update = moment_new / (jnp.sqrt(second_new) + epsilon) + weight_decay * master_weight
    squares = jnp.stack([jnp.sum(master_weight * master_weight, axis=1), jnp.sum(update * update, axis=1)])
    norms = jnp.sqrt(lax.psum(squares, "y"))
    trust = norms[0] / (norms[1] + epsilon)
    return moment_new, second_new, trust[:, None] * update


def solution(mesh):
    fine = Mesh(mesh.devices.reshape(NZ, NX, 2, 4), DP + ("y",))
    split = P(DP, "y")
    return jax.shard_map(
        shards, mesh=fine, in_specs=(split, P(DP, None)) + (split,) * 4, out_specs=(split,) * 3, check_vma=False
    )
```

```python
import functools

import jax
import jax.numpy as jnp
from jax import lax
from jax.experimental import pallas as pl
from jax.experimental.pallas import tpu as pltpu
from jax.sharding import Mesh, PartitionSpec as P

beta_first = 0.9
beta_second = 0.999
weight_decay = 0.01
epsilon = 1e-06

DP = ("z", "x", "c")
NZ, NX = 8, 4
SIZE = {"z": NZ, "x": NX}
COLS_Z = 1280


def dot(lhs_ref, rhs_ref, z, start, cols):
    lhs = lhs_ref[:, pl.ds(pl.multiple_of(z * 256, 256), 256)]
    rhs = rhs_ref[:, start : start + cols]
    return lax.dot_general(lhs, rhs, (((0,), (0,)), ((), ())), preferred_element_type=jnp.float32)


def near_x(x, c):
    return [(lax.rem(x + k, NX), c) for k in range(NX)]


def product_z_kernel(hops, cols, where_ref, lhs_ref, rhs_ref, keep_ref, send_ref, acc):
    z, x, c = where_ref[0], where_ref[1], where_ref[2]
    s = 1 - 2 * c
    near, far = near_x(x, c), near_x(x, 1 - c)

    def put(ref, at, groups):
        for i, (gx, gc) in enumerate(groups):
            row = pl.multiple_of(gx * 64 + gc * 32, 32)
            ref[at + i] = acc[pl.ds(row, 32), :]

    at = 0
    for hop in hops:
        acc[...] = dot(lhs_ref, rhs_ref, lax.rem(z + s * hop + NZ, NZ), 0, cols)
        if hop in (0, NZ // 2):
            put(keep_ref, at, near)
            put(send_ref, at, far)
            at += 4
        else:
            put(keep_ref, at, near + far)
            acc[...] = dot(lhs_ref, rhs_ref, lax.rem(z - s * hop + NZ, NZ), 0, cols)
            put(send_ref, at, far + near)
            at += 8


def product_far_kernel(
    cols, where_ref, lhs_hbm, rhs_hbm, lhs_ref, rhs_ref, keep_ref, send_ref, acc, lhs_sems, rhs_sems
):
    z, x, c = where_ref[0], where_ref[1], where_ref[2]
    far = lax.rem(z + NZ // 2, NZ)

    def bring(hbm, ref, part, sem):
        copy = pltpu.make_async_copy(hbm.at[:, part], ref.at[:, part], sem)
        copy.start()
        return copy

    first = bring(rhs_hbm, rhs_ref, pl.ds(0, cols), rhs_sems.at[0])
    blocks = [
        bring(lhs_hbm, lhs_ref, pl.ds(pl.multiple_of(lax.rem(far + k, NZ) * 256, 256), 256), lhs_sems.at[k])
        for k in range(NZ)
    ]
    rest = bring(rhs_hbm, rhs_ref, pl.ds(cols, rhs_ref.shape[1] - cols), rhs_sems.at[1])
    first.wait()
    blocks[0].wait()
    acc[...] = dot(lhs_ref, rhs_ref, far, 0, cols)
    for ref, core in ((keep_ref, c), (send_ref, 1 - c)):
        for i, (gx, gc) in enumerate(near_x(x, core)):
            ref[i] = acc[pl.ds(pl.multiple_of(gx * 64 + gc * 32, 32), 32), :]
    for block in blocks[1:]:
        block.wait()
    rest.wait()


def product_x_kernel(start, cols, where_ref, lhs_ref, rhs_ref, keep2_ref, send2_ref, keep_ref, send_ref, acc):
    z, x, c = where_ref[0], where_ref[1], where_ref[2]
    s = 1 - 2 * c
    ahead, behind, across = lax.rem(x + s + NX, NX), lax.rem(x - s + NX, NX), lax.rem(x + 2, NX)

    def rows(gx, gc):
        return acc[pl.ds(pl.multiple_of(gx * 64 + gc * 32, 32), 32), :]

    def put(slot, group, near):
        if near:
            keep_ref[slot] = rows(ahead, group)
            send_ref[8 + slot] = rows(behind, group)
            keep2_ref[slot] = rows(across, group)
            keep_ref[16 + slot] = rows(x, group)
        else:
            keep_ref[8 + slot] = rows(ahead, group)
            send_ref[slot] = rows(behind, group)
            send2_ref[slot] = rows(across, group)
            send_ref[16 + slot] = rows(x, group)

    @pl.loop(0, NZ)
    def _(t):
        acc[...] = dot(lhs_ref, rhs_ref, lax.rem(z + s * t + NZ, NZ), start, cols)

        @pl.when(jnp.logical_and(t > 0, t < 4))
        def _():
            put(2 * t - 2, c, True)
            put(2 * t - 1, 1 - c, True)

        @pl.when(t > 4)
        def _():
            put(14 - 2 * t, 1 - c, False)
            put(15 - 2 * t, c, False)

        @pl.when(jnp.logical_or(t == 0, t == 4))
        def _():
            slot = jnp.where(t == 4, 6, 7)
            put(slot, c, True)
            put(slot, 1 - c, False)


VMEM = pl.BlockSpec(memory_space=pltpu.VMEM)


def product(kernel, groups, cols, rows, where, grad_out, attn_out):
    return pl.pallas_call(
        kernel,
        in_specs=[pl.BlockSpec(memory_space=pltpu.SMEM), VMEM, VMEM],
        out_specs=[VMEM] * len(groups),
        out_shape=[jax.ShapeDtypeStruct((g, 32, cols), jnp.float32) for g in groups],
        scratch_shapes=[pltpu.VMEM((256, cols), jnp.float32)],
        compiler_params=pltpu.CompilerParams(vmem_limit_bytes=VLIM),
        cost_estimate=pl.CostEstimate(flops=COST * rows * cols, bytes_accessed=COST * rows, transcendentals=0),
    )(where, grad_out, attn_out)


def product_far(where, grad_out, attn_out):
    hbm = pl.BlockSpec(memory_space=pltpu.HBM)
    return pl.pallas_call(
        functools.partial(product_far_kernel, COLS_Z),
        in_specs=[pl.BlockSpec(memory_space=pltpu.SMEM), hbm, hbm],
        out_specs=[VMEM] * 4,
        out_shape=[jax.ShapeDtypeStruct(v.shape, v.dtype) for v in (grad_out, attn_out)]
        + [jax.ShapeDtypeStruct((4, 32, COLS_Z), jnp.float32)] * 2,
        scratch_shapes=[
            pltpu.VMEM((256, COLS_Z), jnp.float32),
            pltpu.SemaphoreType.DMA((NZ,)),
            pltpu.SemaphoreType.DMA((2,)),
        ],
        compiler_params=pltpu.CompilerParams(vmem_limit_bytes=VFAR),
        cost_estimate=pl.CostEstimate(flops=COST * 256 * COLS_Z, bytes_accessed=COST * 256, transcendentals=0),
    )(where, grad_out, attn_out)


VFAR = 43 << 20
VLIM = 24 << 20
COST = 1


def other_core(value):
    return lax.ppermute(value, "c", [(0, 1), (1, 0)])


def onward(value, axis):
    n = SIZE[axis]
    return lax.ppermute(value, (axis, "c"), [(2 * i + c, 2 * ((i + 1 - 2 * c) % n) + c) for i in range(n) for c in range(2)])


def shift(value, axis, by):
    n = SIZE[axis]
    return lax.ppermute(value, axis, [(i, (i + by) % n) for i in range(n)])


def onward_apart(value, axis):
    n, half = SIZE[axis], value.shape[0] // 2
    cross = [(2 * i + c, 2 * ((i + 1 - 2 * c) % n) + 1 - c) for i in range(n) for c in range(2)]
    return onward(value[:half], axis) + lax.ppermute(value[half:], (axis, "c"), cross)


def at_front(part, whole):
    return lax.pad(part, jnp.float32(0), [(0, whole - part.shape[0], 0), (0, 0, 0), (0, 0, 0)])


def sum_over(tile, axes, n):
    copies = jnp.broadcast_to(tile[None], (n,) + tile.shape)
    return jnp.sum(lax.all_to_all(copies, axes, 0, 0, tiled=True), axis=0)


def after(value, *others):
    return lax.optimization_barrier((value, others))[0]


def shards(attn_out, grad_out, grad_acc, master_weight, moment_m, moment_v):
    entry_count = 2048 * 8192
    where = jnp.stack([lax.axis_index(a) for a in DP]).astype(jnp.int32)

    def product_z(where, hops):
        groups = sum(4 if hop in (0, NZ // 2) else 8 for hop in hops)
        return product(
            functools.partial(product_z_kernel, hops, COLS_Z), [groups] * 2, COLS_Z, groups * 64, where, grad_out, attn_out
        )

    def both(pair):
        return pair[0] + pair[1]

    cols_x = attn_out.shape[1] - COLS_Z

    def add(here, moving):
        return here + (moving if moving.shape == here.shape else at_front(moving, here.shape[0]))

    cuts = (slice(0, 640), slice(640, COLS_Z))

    def hop_z(pair, parts):
        ahead = add(both(pair)[:8, :, cuts[0]], parts[0])
        return ahead, add(both(pair)[:8, :, cuts[1]], after(parts[1], ahead))

    grad_out, attn_out, keep4, send4 = product_far(where, grad_out, attn_out)
    pair4 = (keep4, other_core(send4))
    pair3 = product_z(after(where, pair4[0]), (3,))
    pair3 = (pair3[0], other_core(pair3[1]))
    first_z = lax.optimization_barrier(both(pair4))
    keep_far, send_far, keep_x, send_x = product(
        functools.partial(product_x_kernel, COLS_Z, cols_x),
        [8, 8, 24, 24], cols_x, 2048, after(where, pair3[0], first_z), grad_out, attn_out,
    )
    pair2 = product_z(after(where, keep_far), (2,))
    next_z = add(both(pair3)[:8], after(onward(first_z, "z"), pair2[0]))
    far_x = (keep_far, after(other_core(send_far), next_z))
    pair2 = (pair2[0], other_core(pair2[1]))
    first_x = lax.optimization_barrier(both(far_x))
    pair_x = (keep_x, other_core(after(send_x, first_x)))
    pair1 = product_z(after(where, pair2[0], first_x), (1, 0))
    pair1 = (pair1[0], other_core(pair1[1]))

    x = after(onward(first_x, "x"), pair1[0])
    x = add(both(pair_x)[:16], x)
    next_z = after(onward(next_z, "z"), x)
    z = [next_z[..., cut] for cut in cuts]
    for pair in (pair2, pair1):
        z = [onward(part, "z") for part in hop_z(pair, z)]
    sum_x = onward_apart(x, "x") + both(pair_x)[16:24]

    moving = onward(sum_x[6:7], "z")
    far = [other_core(z[0][4:])]
    z[1] = after(z[1], moving)
    moving = add(sum_x[4:6], after(moving, z[1]))
    far.append(other_core(after(z[1][4:], moving)))
    sum_z = jnp.concatenate([z[i][:4] + far[i] for i in range(2)], axis=2) + both(pair1)[8:12]
    batch_z = sum_z[0] + sum(shift(sum_z[k], "x", k) for k in (1, 2, 3))
    moving = onward(moving, "z")
    moving = onward(sum_x[2:4] + moving, "z")
    batch_x = onward_apart(sum_x[0:2] + after(moving, batch_z), "z")[0] + sum_x[7]
    gradient = grad_acc + jnp.concatenate([batch_z, batch_x], axis=1)

    energy = jnp.sum((gradient * gradient).reshape(4, 8, 16, 128), axis=(0, 2))
    energy = sum_over(sum_over(energy, ("z", "c"), 16), ("x", "y"), 16)
    divisor = jnp.sqrt(jnp.sum(energy) / entry_count + epsilon)
    clipped = gradient / divisor
    moment_new = beta_first * moment_m + (1.0 - beta_first) * clipped
    second_new = beta_second * moment_v + (1.0 - beta_second) * clipped * clipped
    update = moment_new / (jnp.sqrt(second_new) + epsilon) + weight_decay * master_weight
    squares = jnp.stack([jnp.sum(master_weight * master_weight, axis=1), jnp.sum(update * update, axis=1)])
    norms = jnp.sqrt(lax.psum(squares, "y"))
    trust = norms[0] / (norms[1] + epsilon)
    return moment_new, second_new, trust[:, None] * update


def solution(mesh):
    fine = Mesh(mesh.devices.reshape(NZ, NX, 2, 4), DP + ("y",))
    split = P(DP, "y")
    return jax.shard_map(
        shards, mesh=fine, in_specs=(split, P(DP, None)) + (split,) * 4, out_specs=(split,) * 3, check_vma=False
    )
```
